128 devices in a mesh: exa: 8 (over z, core), exb: 16 (over x, y).
Axes of the slice: x: 4, y: 4, z: 4, core: 2. Of those that a mesh axis runs over, the one named last changes fastest.
Arguments:
- features: float32 [1048576, 128], P(('exa', 'exb')), may hold values from -6 to 6
- sign_bits: int32 [1048576], P(('exa', 'exb')), may hold values from 0 to 1
- sample_device: int32 [65536, 1], replicated, may hold values from 0 to 127; in each aligned block of 512 rows (0 to 511, 512 to 1023, ...) at most 8 rows name the same one
- sample_offset: int32 [65536], replicated, may hold values from 0 to 8191, as said below
Outputs:
- q_rows: float32 [65536, 128], P(('exa', 'exb'))
- upper_factor: float32 [128, 128], replicated
The draws below stay inside these ranges and needn't reach their ends.
Inputs may be any that keep to these rules, and one draw needn't show every extreme that they name: `sample_device`: within each aligned block of 512 rows no value appears more than 8 times. `sample_offset`: within each aligned block of 512 rows, at most 8 values fall into any one range of 64 consecutive offsets that starts at a multiple of 64, and in every block some range holds exactly 8.
All inputs are finite; a program needn't handle non-finite values.
Results may differ from the reference program's by a relative error of at most 0.000071.
Values sent between devices are 32-bit elements; how exact they have to be, the bound alone decides.
A program may use at most 64 MiB of HBM per device.

```python
import math
import jax
import jax.numpy as jnp
import numpy as np
from jax import lax

F = 128
L_DEV = 8192
K_DEV = 512
EXAMPLES = 1048576
SAMPLES = 65536
MOST = 8
N_EXA = 8
N_EXB = 16
DEVICES = 128


def draw_sample_offset(key, part):
    group_rows = L_DEV // DEVICES
    capacity = max(4, 2 * K_DEV // DEVICES)

    def one_block(block_key):
        first_key, second_key, third_key, fourth_key = jax.random.split(block_key, 4)
        heavy = jax.random.randint(first_key, (), 0, DEVICES).astype(jnp.int32)
        others = jnp.arange((DEVICES - 1) * capacity, dtype=jnp.int32) // capacity
        others = (heavy + 1 + others) % DEVICES
        others = jax.random.permutation(second_key, others)[:K_DEV - capacity]
        groups = jnp.concatenate([jnp.full((capacity,), heavy, jnp.int32), others.astype(jnp.int32)])
        groups = jax.random.permutation(third_key, groups)
        within = jax.random.randint(fourth_key, (K_DEV,), 0, group_rows).astype(jnp.int32)
        return groups * group_rows + within
    block_keys = jax.random.split(jax.random.fold_in(key, 7), DEVICES)
    return jax.vmap(one_block)(block_keys).reshape(-1).astype(jnp.int32)


def with_ends(array, own_key, low, largest):
    longest = array.shape.index(max(array.shape))
    spots = []
    for shift in (0, 1):
        where = [jax.random.randint(jax.random.fold_in(own_key, axis), (), 0, length) for axis, length in enumerate(array.shape)]
        where[longest] = (where[longest] + shift) % array.shape[longest]
        spots.append(tuple(where))
    return array.at[spots[0]].set(low).at[spots[1]].set(largest)


def block_scale(key, dims, cuts, least, largest):
    loudness, own = 1.0, jax.random.fold_in(key, 6)
    for position, shards_of in cuts:
        heights = jnp.exp(jax.random.uniform(jax.random.fold_in(own, position), (shards_of,), jnp.float32, least / len(cuts), largest / len(cuts)))
        loudness = loudness * jnp.repeat(heights, dims[position] // shards_of).reshape([-1 if axis == position else 1 for axis in range(len(dims))])
    return loudness


def routed_block(rng, own, number, rows, number_of, top, most, slope):
    order = jax.random.permutation(rng, number_of)
    crowded, usual = shares(number_of, rows * top, most, slope, True), shares(number_of, rows * top, most, slope, False)
    places = jnp.arange(number_of)

    def named(lengths, rotation):
        used = int((lengths > 0).sum())
        fixed = max(1, used // 4)
        moved = fixed + (places - fixed + rotation * (used - fixed)) % max(1, number_of - fixed)
        return jnp.zeros((number_of,), jnp.int32).at[order[jnp.where(places < fixed, places, moved)]].set(jnp.asarray(lengths, jnp.int32))

    lengths = jnp.where(number % 4 == 0, named(crowded, number // 4), named(usual, number - number // 4 - 1))
    mixed = jax.random.permutation(jax.random.fold_in(own, 3), number_of)
    giver, receiver = mixed[0:number_of // 2 * 2:2], mixed[1:number_of // 2 * 2:2]
    margin = jnp.minimum(lengths[giver] - 1, most - lengths[receiver]) // 2
    margin = jnp.where((giver == order[0]) | (receiver == order[0]) | (lengths[receiver] == 0), 0, jnp.maximum(margin, 0))
    moved = jax.random.randint(jax.random.fold_in(own, 4), (number_of // 2,), 0, 1 << 20) % (margin + 1)
    lengths = lengths.at[giver].add(-moved).at[receiver].add(moved)
    items = jnp.searchsorted(jnp.cumsum(lengths), jnp.arange(rows * top), side="right").astype(jnp.int32)
    table = items.reshape(top, rows).T
    table = table[jax.random.permutation(jax.random.fold_in(own, 1), rows)]
    rotation = jax.random.randint(jax.random.fold_in(own, 2), (rows, 1), 0, top)
    return jnp.take_along_axis(table, (jnp.arange(top)[None, :] + rotation) % top, axis=1)


def shares(count, total, bound, slope, full):
    portions = [(1 << 20) // math.isqrt(rank ** slope) + 1 for rank in range(1, count + 1)]
    largest = bound if full else min(bound, max(-(-total // count), total * portions[0] // sum(portions)))
    least = 1 if total - largest >= count - 1 else 0
    holding, spare = [largest] + [least] * (count - 1), total - largest - least * (count - 1)
    while spare > 0:
        candidates = [i for i in range(1, count) if holding[i] < largest] or [i for i in range(1, count) if holding[i] < bound]
        whole, remaining = sum([portions[i] for i in candidates]), spare
        for i in candidates:
            more = min(bound - holding[i], max(1, remaining * portions[i] // whole), spare)
            holding[i] = holding[i] + more
            spare = spare - more
    return np.array(holding)


def normal_values(own_key, shape, width, bound, cuts=(), kind=jnp.bfloat16):
    entries = width * jax.random.normal(own_key, shape, jnp.float32)
    if cuts:
        entries = entries * block_scale(own_key, shape, cuts, -0.22, 0.18)
    return jnp.clip(entries, -bound, bound).astype(kind)


def setup_inputs(seed: int = 0) -> dict:
    key_of = jax.random.split(jax.random.key(seed), 5)
    features = normal_values(key_of[0], (EXAMPLES, F), 1.0, 6.0, ((0, 128),), jnp.float32)
    sign_bits = with_ends(jax.random.randint(key_of[1], (EXAMPLES,), 0, 2), jax.random.fold_in(key_of[1], 1), 0, 1).astype(jnp.int32)
    sample_device_keys = jax.random.split(jax.random.fold_in(key_of[2], 1), SAMPLES // K_DEV)
    sample_device_turns = jax.random.permutation(jax.random.fold_in(key_of[2], 3), SAMPLES // K_DEV)
    sample_device = jax.vmap(lambda own, number: routed_block(jax.random.fold_in(key_of[2], 2), own, number, K_DEV, DEVICES, 1, MOST, 2))(sample_device_keys, sample_device_turns).reshape((SAMPLES, 1))
    sample_offset = draw_sample_offset(jax.random.fold_in(key_of[4], 71), 0)
    return {"features": features, "sign_bits": sign_bits, "sample_device": sample_device, "sample_offset": sample_offset}


def hadamard_table(order_size):
    index = jnp.arange(order_size, dtype=jnp.int32)
    common = index[:, None] & index[None, :]
    parity = jnp.zeros((order_size, order_size), jnp.int32)
    for bit_pos in range(max(order_size.bit_length(), 1)):
        parity = parity + (common >> bit_pos & 1)
    return (1 - 2 * (parity % 2)).astype(jnp.float32)

def reference(features, sign_bits, sample_device, sample_offset):
    highest = lax.Precision.HIGHEST
    sign_values = (2 * sign_bits - 1).astype(jnp.float32)
    signed = features * sign_values[:, None]
    blocks = L_DEV // 128
    grid = signed.reshape(N_EXA, N_EXB, blocks, 128, F)
    grid = jnp.einsum('ka,abcdf->kbcdf', hadamard_table(N_EXA), grid, precision=highest)
    grid = jnp.einsum('kb,abcdf->akcdf', hadamard_table(N_EXB), grid, precision=highest)
    grid = jnp.einsum('kc,abcdf->abkdf', hadamard_table(blocks), grid, precision=highest)
    grid = jnp.einsum('kd,abcdf->abckf', hadamard_table(128), grid, precision=highest)
    transformed = grid.reshape(EXAMPLES, F) / math.sqrt(EXAMPLES)
    row_index = (sample_device[:, 0] * L_DEV + sample_offset).astype(jnp.int32)
    sketch = jnp.take(transformed, row_index, axis=0)
    gram = jnp.dot(sketch.T, sketch, precision=highest) / SAMPLES
    upper_factor = jnp.linalg.cholesky(gram).T
    q_rows = lax.linalg.triangular_solve(upper_factor, sketch, left_side=False, lower=False, transpose_a=False)
    return (q_rows, upper_factor)
```

```python
import math

import jax
import jax.numpy as jnp
from jax import lax
from jax.experimental import pallas as pl
from jax.experimental.pallas import tpu as pltpu
from jax.sharding import PartitionSpec as P


def hadamard_table(order_size):
    index = jnp.arange(order_size, dtype=jnp.int32)
    common = index[:, None] & index[None, :]
    parity = jnp.zeros((order_size, order_size), jnp.int32)
    for bit_pos in range(max(order_size.bit_length(), 1)):
        parity = parity + (common >> bit_pos & 1)
    return (1 - 2 * (parity % 2)).astype(jnp.float32)


def factor(gram_ref, upper_ref, inverse_ref, work):
    width = 128
    rows = lax.broadcasted_iota(jnp.int32, (8, width), 0)
    lanes = lax.broadcasted_iota(jnp.int32, (8, width), 1)
    work[:, :width] = gram_ref[...]
    work[:, width:] = (
        lax.broadcasted_iota(jnp.int32, (width, width), 0)
        == lax.broadcasted_iota(jnp.int32, (width, width), 1)
    ).astype(jnp.float32)
    for panel in range(width // 8):
        low = 8 * panel
        left = work[low : low + 8, :width]
        right = work[low : low + 8, width:]
        cols = [
            jnp.broadcast_to(left[:, low + j : low + j + 1], (8, width)) for j in range(8)
        ]
        pivots = jnp.ones((8, width), jnp.float32)
        for i in range(8):
            pivot = jnp.broadcast_to(cols[i][i : i + 1, :], (8, width))
            pivots = jnp.where(rows == i, pivot, pivots)
            if i < 7:
                scaled = jnp.where(rows > i, cols[i] / pivot, 0.0)
                for j in range(i + 1, 8):
                    cols[j] = cols[j] - scaled * cols[j][i : i + 1, :]
                left = left - scaled * left[i : i + 1, :]
                right = right - scaled * right[i : i + 1, :]
        root = lax.rsqrt(pivots)
        root = root * (1.5 - 0.5 * pivots * root * root)
        left = jnp.where(lanes >= rows + low, left * root, 0.0)
        right = right * root
        upper_ref[low : low + 8, :] = left
        inverse_ref[low : low + 8, :] = right
        if low + 8 < width:
            change = lax.dot_general(
                left,
                jnp.concatenate([left, right], axis=1),
                (((0,), (0,)), ((), ())),
                precision=lax.Precision.HIGHEST,
                preferred_element_type=jnp.float32,
            )
            work[low + 8 :, :] = work[low + 8 :, :] - change[low + 8 :, :]


def factor_call(gram):
    return pl.pallas_call(
        factor,
        out_shape=[jax.ShapeDtypeStruct((128, 128), jnp.float32)] * 2,
        scratch_shapes=[pltpu.VMEM((128, 256), jnp.float32)],
    )(gram)


def slot_select(from_here, values, slot_count):
    own_count = from_here.shape[1]
    positions = jnp.arange(own_count, dtype=jnp.int32)
    before_mask = (positions[:, None] < positions[None, :]).astype(jnp.float32)
    slot_rank = jnp.dot(
        from_here.astype(jnp.float32), before_mask, precision=lax.Precision.HIGHEST
    ).astype(jnp.int32)
    slot_ids = jnp.arange(slot_count, dtype=jnp.int32)
    slot_hit = from_here[:, :, None] & (slot_rank[:, :, None] == slot_ids[None, None, :])
    picked = jnp.sum(jnp.where(slot_hit, values[:, :, None], 0), axis=1)
    slot_valid = jnp.any(slot_hit, axis=1).astype(jnp.float32)
    return (picked, slot_valid)


def rank_within(keys_mine):
    own_count = keys_mine.shape[0]
    positions = jnp.arange(own_count, dtype=jnp.int32)
    same_key = keys_mine[:, None] == keys_mine[None, :]
    earlier_rows = positions[None, :] < positions[:, None]
    return jnp.sum((same_key & earlier_rows).astype(jnp.int32), axis=1)


def per_device(features, sign_bits, sample_device, sample_offset):
    highest = lax.Precision.HIGHEST
    rows_dev, feat_width = features.shape
    n_outer = lax.axis_size("exa")
    n_inner = lax.axis_size("exb")
    n_all = n_outer * n_inner
    myself = lax.axis_index("exa") * n_inner + lax.axis_index("exb")
    sign_values = (2 * sign_bits - 1).astype(jnp.float32)
    signed = features * sign_values[:, None]
    blocks = rows_dev // 128
    local_grid = signed.reshape(blocks, 128, feat_width)
    local_grid = jnp.einsum("kj,bjf->bkf", hadamard_table(128), local_grid, precision=highest)
    local_grid = jnp.einsum("kb,bjf->kjf", hadamard_table(blocks), local_grid, precision=highest)
    signed_local = local_grid.reshape(rows_dev, feat_width)
    piece_rows = rows_dev // n_all
    all_table = hadamard_table(n_all)
    mixed = jnp.einsum(
        "ks,spf->kpf",
        all_table,
        lax.all_to_all(
            signed_local.reshape(n_all, piece_rows, feat_width),
            ("exa", "exb"),
            split_axis=0,
            concat_axis=0,
            tiled=True,
        ),
        precision=highest,
    )
    scale = 1.0 / math.sqrt(rows_dev * n_all)
    total_samples = sample_device.shape[0]
    own_count = total_samples // n_all
    source_all = sample_device[:, 0].reshape(n_all, own_count)
    offset_all = sample_offset.reshape(n_all, own_count)
    offset_mine = lax.dynamic_slice_in_dim(sample_offset, myself * own_count, own_count)
    group_rows = rows_dev // n_all
    group_slots = max(4, 2 * own_count // n_all)
    group_all = offset_all // group_rows
    within_all = offset_all % group_rows
    group_mine = offset_mine // group_rows
    flat_all = source_all * group_rows + within_all
    held_flat = mixed.reshape(n_all * group_rows, feat_width)
    from_here = group_all == myself
    picked_rows, slot_valid = slot_select(from_here, flat_all, group_slots)
    outgoing = jnp.take(held_flat, picked_rows.reshape(-1), axis=0) * (
        slot_valid.reshape(-1)[:, None] * scale
    )
    outgoing = outgoing.reshape(n_all, group_slots, feat_width)
    received = lax.all_to_all(outgoing, ("exa", "exb"), split_axis=0, concat_axis=0, tiled=True)
    rank_mine = rank_within(group_mine)
    sketch = jnp.take(
        received.reshape(n_all * group_slots, feat_width),
        group_mine * group_slots + rank_mine,
        axis=0,
    )
    gram_local = jnp.dot(sketch.T, sketch, precision=highest) / total_samples
    gram = lax.psum(gram_local, ("exa", "exb"))
    upper_factor, inverse = factor_call(gram)
    q_rows = jnp.dot(sketch, inverse.T, precision=highest)
    return (q_rows, upper_factor)


def solution(mesh):
    placed = (P(("exa", "exb"), None), P(("exa", "exb")), P(), P())
    return jax.shard_map(
        per_device,
        mesh=mesh,
        in_specs=placed,
        out_specs=(P(("exa", "exb"), None), P()),
        check_vma=False,
    )
```

```python
import jax
import jax.numpy as jnp
from jax import lax
from jax.experimental import pallas as pl
from jax.experimental.pallas import tpu as pltpu
from jax.sharding import PartitionSpec as P

MESH = pl.DeviceIdType.MESH
GROUP_BITS = (6, 5, 3, 2, 1, 0)
STEPS = (96, 32, 12, 4, 3, 1)
CORE_BIT = 4
FIRST = (5, 0, 1, 3, 4, 2, 3, 4, 5, 5, 0, 2, 1, 1, 1, 0)
ORDER = (
    (0, 0), (1, 0), (2, 0), (3, 0), (4, 0), (5, 0), (6, 0), (7, 0), (0, 1), (1, 1),
    (2, 1), (3, 1), (4, 1), (5, 1), (8, 1), (10, 1), (12, 1), (6, 1), (7, 1), (11, 1),
    (9, 1), (15, 1), (13, 1), (5, 2), (3, 2), (2, 2), (4, 2), (0, 2), (14, 1), (11, 2),
    (6, 2), (12, 2), (7, 2), (8, 2), (1, 2), (2, 3), (5, 3), (13, 2), (3, 3), (9, 2),
    (10, 2), (12, 3), (11, 3), (14, 2), (6, 3), (4, 3), (15, 2), (13, 3), (2, 4), (1, 3),
    (5, 4), (7, 3), (0, 3), (14, 3), (12, 4), (10, 3), (11, 4), (3, 4), (8, 3), (1, 4),
    (13, 4), (15, 3), (2, 5), (6, 4), (9, 3), (10, 4), (14, 4), (0, 4), (12, 5), (5, 5),
    (4, 4), (15, 4), (1, 5), (8, 4), (13, 5), (11, 5), (7, 4), (0, 5), (10, 5), (9, 4),
    (14, 5), (2, 6), (3, 5), (8, 5), (15, 5), (4, 5), (1, 6), (12, 6), (6, 5), (9, 5),
    (0, 6), (7, 5), (10, 6), (13, 6), (5, 6), (4, 6), (8, 6), (3, 6), (15, 6), (14, 6),
    (11, 6), (7, 6), (9, 6), (6, 6),
)
SCALE = 1.0 / 1024.0


def bit_of(number, bit):
    return (number // (1 << bit)) % 2


def flip(number, mask):
    for bit in range(7):
        if mask >> bit & 1:
            number = number + (1 << bit) * (1 - 2 * bit_of(number, bit))
    return number


def group_of(device):
    out = 0
    for bit in range(7):
        value = bit_of(device, bit)
        if bit in (0, 2, 5):
            above = bit_of(device, bit + 1)
            value = value + above - 2 * value * above
        out = out + value * (1 << bit)
    return out


def place_of(device):
    return (device // 16, device % 16)


def sublane_hadamard(tile, rows):
    for step in (4, 2, 1):
        high = (rows // step) % 2 == 1
        if step == 4:
            other = pltpu.roll(tile, 4, 0)
        else:
            other = jnp.where(high, pltpu.roll(tile, step, 0), pltpu.roll(tile, 8 - step, 0))
        tile = jnp.where(high, other - tile, tile + other)
    return tile


def factor(gram, upper_ref, inverse_ref, work, beside):
    width, size = 128, 16
    rows = lax.broadcasted_iota(jnp.int32, (8, width), 0)
    lanes = lax.broadcasted_iota(jnp.int32, (8, width), 1)
    work[:, :width] = gram
    work[:, width:] = (
        lax.broadcasted_iota(jnp.int32, (width, width), 0)
        == lax.broadcasted_iota(jnp.int32, (width, width), 1)
    ).astype(jnp.float32)
    both = work[:size, :]
    for panel in range(width // size):
        beside(panel)
        low, end = size * panel, size * (panel + 1)
        left = [both[8 * t : 8 * t + 8, :width] for t in range(2)]
        right = [both[8 * t : 8 * t + 8, width:] for t in range(2)]
        cols = [
            [jnp.broadcast_to(tile[:, low + j : low + j + 1], (8, width)) for tile in left]
            for j in range(size)
        ]
        pivots = [jnp.ones((8, width), jnp.float32) for _ in range(2)]
        for i in range(size):
            own, row = divmod(i, 8)
            pivot = jnp.broadcast_to(cols[i][own][row : row + 1, :], (8, width))
            pivots[own] = jnp.where(rows == row, pivot, pivots[own])
            left_row, right_row = left[own][row : row + 1, :], right[own][row : row + 1, :]
            col_row = [cols[j][own][row : row + 1, :] for j in range(size)]
            for t in range(own, 2):
                if t == own and row == 7:
                    continue
                scaled = cols[i][t] / pivot
                if t == own:
                    scaled = jnp.where(rows > row, scaled, 0.0)
                for j in range(i + 1, size):
                    cols[j][t] = cols[j][t] - scaled * col_row[j]
                left[t] = left[t] - scaled * left_row
                right[t] = right[t] - scaled * right_row
        for t in range(2):
            root = lax.rsqrt(pivots[t])
            root = root * (1.5 - 0.5 * pivots[t] * root * root)
            left[t] = jnp.where(lanes >= rows + (low + 8 * t), left[t] * root, 0.0)
            right[t] = right[t] * root
            upper_ref[low + 8 * t : low + 8 * t + 8, :] = left[t]
            inverse_ref[low + 8 * t : low + 8 * t + 8, :] = right[t]
        if end < width:
            top = jnp.concatenate(left, axis=0)
            turned = top.T
            top = jnp.concatenate([top, jnp.concatenate(right, axis=0)], axis=1)
            both = work[end : end + size, :] - dot_exact(turned[end : end + size, :], top, ((1,), (0,)))
            if end + size < width:
                work[end + size :, :] = work[end + size :, :] - dot_exact(
                    turned[end + size :, :], top, ((1,), (0,))
                )


def dot_exact(a, b, contract):
    return lax.dot_general(
        a,
        b,
        (contract, ((), ())),
        precision=lax.Precision.HIGHEST,
        preferred_element_type=jnp.float32,
    )


def sample_tables(group, device, device_ref, offset_ref, give_ref, take_ref):
    shape = (512, 128)
    offsets = offset_ref[...]
    sources = device_ref[...]
    here = offsets // 64 == group
    mine = jnp.where(here, 1.0, 0.0)
    square = (128, 128)
    first = lax.broadcasted_iota(jnp.int32, square, 0)
    second = lax.broadcasted_iota(jnp.int32, square, 1)
    before = jnp.where(first < second, 1.0, 0.0).astype(jnp.bfloat16)
    ones = jnp.ones(square, jnp.bfloat16)

    def plain(a, b):
        return lax.dot_general(
            a.astype(jnp.bfloat16),
            b.astype(jnp.bfloat16),
            (((1,), (0,)), ((), ())),
            preferred_element_type=jnp.float32,
        )

    wide = (512, 512)
    later = lax.broadcasted_iota(jnp.int32, wide, 0)
    earlier = lax.broadcasted_iota(jnp.int32, wide, 1)
    lines = jnp.where((later // 4 == earlier // 4) & (earlier < later), 1.0, 0.0)
    rank = plain(mine, before) + plain(lines, plain(mine, ones))
    value = (sources * 8192 + offsets + 1).astype(jnp.float32)
    lanes = lax.broadcasted_iota(jnp.int32, shape, 1)
    found = jnp.zeros(shape, jnp.float32)
    for k in range(8):
        chosen = jnp.where(here & (rank == float(k)), value, 0.0)
        found = jnp.where(lanes == k, jnp.sum(chosen, axis=1, keepdims=True), found)
    blocks = jnp.where(
        lax.broadcasted_iota(jnp.int32, shape, 0) // 4
        == lax.broadcasted_iota(jnp.int32, shape, 1),
        1.0,
        0.0,
    )
    slots = dot_exact(found, blocks, ((0,), (0,)))[0:8, :].astype(jnp.int32)
    full = slots - 1
    source = full // 8192
    offset = full % 8192
    natural = jnp.zeros_like(full)
    for link in range(6):
        step = STEPS[link]
        sign = jnp.zeros_like(full)
        for bit in range(7):
            if step >> bit & 1:
                sign = sign + (source // (1 << bit)) % 2
        natural = natural + (sign % 2) * (1 << (5 - link))
    part = 2 * ((offset // 8) % 8) + (source // (1 << CORE_BIT)) % 2
    spot = jnp.zeros_like(full)
    for number in range(16):
        turn = FIRST[number]
        turned = (natural % (1 << (6 - turn))) * (1 << turn) + natural // (1 << (6 - turn))
        spot = jnp.where(part == number, turned, spot)
    row = part * 512 + spot * 8 + offset % 8
    give_ref[...] = jnp.clip(jnp.where(slots > 0, row, 8192), 0, 8192)

    total = jnp.zeros(square, jnp.float32)
    for q in range(4):
        groups = offset_ref[pl.ds(4 * device + q, 1), :] // 64
        same = jnp.where(groups == first, 1.0, 0.0)
        count = plain(same, before) + total
        place = jnp.sum(same * count, axis=0, keepdims=True)
        take_ref[q : q + 1, :] = jnp.clip(groups * 8 + place.astype(jnp.int32), 0, 1023)
        total = total + plain(same, ones)


def kernel(
    features_ref,
    bits_hbm,
    device_hbm,
    offset_hbm,
    sketch,
    inverse,
    upper_ref,
    bits_ref,
    device_ref,
    offset_ref,
    rows_in,
    signs,
    core_send,
    core_keep,
    core_got,
    send,
    keep,
    got,
    held,
    give_v,
    take_v,
    give,
    take,
    outgoing,
    received,
    gram_part,
    gram_got,
    gram_row,
    gram,
    work,
    in_sem,
    table_sem,
    core_send_sem,
    core_got_sem,
    send_sem,
    got_sem,
    row_sem,
    sum_sem,
):
    device = lax.axis_index("exa") * 16 + lax.axis_index("exb")
    group = group_of(device)
    partners = [flip(device, 1 << CORE_BIT)] + [flip(device, step) for step in STEPS]
    core_sign = (1 - 2 * bit_of(group, CORE_BIT)).astype(jnp.float32)
    link_sign = [(1 - 2 * bit_of(group, bit)).astype(jnp.float32) for bit in GROUP_BITS]

    loads = [
        pltpu.make_async_copy(
            features_ref.at[pl.ds(1024 * c, 1024)], rows_in.at[pl.ds(1024 * c, 1024)], in_sem.at[c]
        )
        for c in range(8)
    ]
    small = [
        pltpu.make_async_copy(bits_hbm, bits_ref, in_sem.at[8]),
        pltpu.make_async_copy(device_hbm, device_ref, in_sem.at[9]),
        pltpu.make_async_copy(offset_hbm, offset_ref, in_sem.at[10]),
    ]
    small[0].start()
    for load in loads:
        load.start()
    small[1].start()
    small[2].start()
    barrier = pltpu.get_barrier_semaphore()
    for partner in partners:
        pl.semaphore_signal(barrier, inc=1, device_id=place_of(partner), device_id_type=MESH)

    small[0].wait()
    bits = (2 * bits_ref[...] - 1).astype(jnp.float32)
    signs[...] = jnp.transpose(jnp.concatenate([bits, bits], axis=0))

    def first_pass(pair):
        def body(low, carry):
            turned = signs[...]
            for half in range(2):
                tiles = []
                for side in range(2):
                    base = pl.multiple_of(2048 * pair + 1024 * side + 128 * low + 64 * half, 64)
                    column = 0
                    some = []
                    for t in range(8):
                        sign = jnp.broadcast_to(
                            turned[64 * half + 8 * t : 64 * half + 8 * t + 8, 8 * side : 8 * side + 1], (8, 128)
                        )
                        some.append(rows_in[pl.ds(pl.multiple_of(base + 8 * t, 8), 8), :] * sign)
                    for step in (1, 2, 4):
                        for t in range(8):
                            if not t & step:
                                a, b = some[t], some[t + step]
                                some[t], some[t + step] = a + b, a - b
                    tiles.append(some)
                spot = 16 * pair + 2 * low + half
                for t in range(8):
                    a, b = tiles[0][t], core_sign * tiles[1][t]
                    core_keep[t, spot] = a + b
                    core_send[t, spot] = a - b
            signs[...] = pltpu.roll(turned, 127, 1)
            return carry

        lax.fori_loop(0, 8, body, 0)

    def core_copy(part):
        return pltpu.make_async_remote_copy(
            src_ref=core_send.at[part],
            dst_ref=core_got.at[part],
            send_sem=core_send_sem.at[part],
            recv_sem=core_got_sem.at[part],
            device_id=place_of(partners[0]),
            device_id_type=MESH,
        )

    for pair in range(4):
        loads[2 * pair].wait()
        loads[2 * pair + 1].wait()
        first_pass(pair)
        if pair < 3:
            signs[...] = pltpu.roll(signs[...], 120, 1)
    pl.semaphore_wait(barrier, 7)
    for part in range(8):
        core_copy(part).start()

    def link_copy(part, stage):
        link = (FIRST[part] + stage - 1) % 6
        return pltpu.make_async_remote_copy(
            src_ref=send.at[part, stage - 1],
            dst_ref=got.at[part, stage - 1],
            send_sem=send_sem.at[part, stage - 1],
            recv_sem=got_sem.at[part, stage - 1],
            device_id=place_of(partners[1 + link]),
            device_id_type=MESH,
        )

    small[1].wait()
    small[2].wait()
    sample_tables(group, device, device_ref, offset_ref, give_v, take_v)
    give_copy = pltpu.make_async_copy(give_v, give, table_sem.at[0])
    take_copy = pltpu.make_async_copy(take_v, take, table_sem.at[1])
    give_copy.start()
    take_copy.start()
    give_copy.wait()
    take_copy.wait()

    lines = lax.broadcasted_iota(jnp.int32, (8, 128), 0)

    def core_stage(part, side):
        number = 2 * part + side
        turn = FIRST[number]
        sign = link_sign[turn]

        def one(rot):
            spot = rot // (1 << turn) + (rot % (1 << turn)) * (1 << (6 - turn))
            a, b = core_keep[part, spot], core_got[part, spot]
            return a + b if side == 0 else core_sign * (a - b)

        def body(step, carry):
            for more in range(4):
                j = 4 * step + more
                a, b = one(j), sign * one(j + 32)
                keep[number, 0, j] = a + b
                send[number, 0, j] = a - b
            return carry

        lax.fori_loop(0, 8, body, 0)

    def link_stage(part, stage):
        link = (FIRST[part] + stage - 1) % 6
        sign, after = link_sign[link], link_sign[(link + 1) % 6]
        old, new = (stage - 1) % 2, stage % 2

        def pair(i):
            a, b = keep[part, old, i], got[part, stage - 1, i]
            return a + b, sign * (a - b)

        def body(step, carry):
            for more in range(4):
                i = 4 * step + more
                for side, (a, b) in enumerate(zip(pair(i), pair(i + 16))):
                    if stage == 2:
                        a, b = sublane_hadamard(a, lines), sublane_hadamard(b, lines)
                    b = after * b
                    keep[part, new, 2 * i + side] = a + b
                    send[part, stage, 2 * i + side] = a - b
            return carry

        lax.fori_loop(0, 4, body, 0)

    def last_stage(part):
        sign = link_sign[(FIRST[part] + 5) % 6] * SCALE

        def body(step, carry):
            for more in range(4):
                i = 4 * step + more
                a, b = keep[part, 1, i], got[part, 5, i]
                base = pl.multiple_of(512 * part + 16 * i, 16)
                held[pl.ds(base, 8), :] = SCALE * (a + b)
                held[pl.ds(pl.multiple_of(base + 8, 8), 8), :] = sign * (a - b)
            return carry

        lax.fori_loop(0, 8, body, 0)

    for part, stage in ORDER:
        if stage == 0:
            core_copy(part).wait_recv()
            for side in range(2):
                core_stage(part, side)
                link_copy(2 * part + side, 1).start()
        else:
            link_copy(part, stage).wait_recv()
            if stage < 6:
                link_stage(part, stage)
                link_copy(part, stage + 1).start()
            else:
                last_stage(part)
    held[8192:8200, :] = jnp.zeros((8, 128), jnp.float32)

    def gather(step, carry):
        for more in range(4):
            to = 4 * step + more
            for k in range(8):
                row = jnp.clip(give[k, to], 0, 8192)
                outgoing[pl.ds(8 * to + k, 1), :] = held[pl.ds(row, 1), :]
        return carry

    lax.fori_loop(0, 32, gather, 0)

    def row_copy(to):
        return pltpu.make_async_remote_copy(
            src_ref=outgoing.at[pl.ds(pl.multiple_of(8 * to, 8), 8)],
            dst_ref=received.at[pl.ds(pl.multiple_of(8 * group, 8), 8)],
            send_sem=row_sem.at[0],
            recv_sem=row_sem.at[1],
            device_id=place_of(to),
            device_id_type=MESH,
        )

    gram_part[...] = dot_exact(outgoing[...], outgoing[...], ((0,), (0,)))

    def part_copy(to):
        return pltpu.make_async_remote_copy(
            src_ref=gram_part.at[pl.ds(to, 1)],
            dst_ref=gram_got.at[pl.ds(device, 1)],
            send_sem=sum_sem.at[0],
            recv_sem=sum_sem.at[1],
            device_id=place_of(to),
            device_id_type=MESH,
        )

    def sum_copy(to):
        return pltpu.make_async_remote_copy(
            src_ref=gram_row,
            dst_ref=gram.at[pl.ds(device, 1)],
            send_sem=sum_sem.at[2],
            recv_sem=sum_sem.at[3],
            device_id=place_of(to),
            device_id_type=MESH,
        )

    exa, exb = lax.axis_index("exa"), lax.axis_index("exb")
    turns = (2, 3, 1, 0)
    lower = {dz: 32 * ((exa // 2 + dz) % 4) for dz in turns}
    middle = {dx: 4 * ((exb // 4 + dx) % 4) for dx in turns}
    upper = {dy: (exb + dy) % 4 for dy in turns}
    cores = (16 * (1 - exa % 2), 16 * (exa % 2))
    shifts = [(z, x, y, c) for z in turns for x in turns for y in turns for c in (0, 1)]
    shifts = sorted(shifts, key=lambda t: -sum(min(v, 4 - v) for v in t[:3]))

    def all_others(copy):
        for z, x, y, c in shifts[:-1]:
            copy(lower[z] + cores[c] + (middle[x] + upper[y])).start()

    def wait_bytes(ref, sem):
        pltpu.make_async_copy(ref, ref, sem).wait()

    all_others(part_copy)
    gram_got[pl.ds(device, 1), :] = gram_part[pl.ds(device, 1), :]
    wait_bytes(gram_got.at[pl.ds(0, 127)], sum_sem.at[1])
    gram_row[...] = jnp.sum(gram_got[...], axis=0, keepdims=True) * (1.0 / 65536.0)
    all_others(sum_copy)
    gram[pl.ds(device, 1), :] = gram_row[...]
    all_others(row_copy)
    received[pl.ds(pl.multiple_of(8 * group, 8), 8), :] = outgoing[
        pl.ds(pl.multiple_of(8 * device, 8), 8), :
    ]

    def take_rows(panel):
        if panel == 4:
            wait_bytes(received.at[pl.ds(0, 1016)], row_sem.at[1])
        if panel >= 4:
            for j in range(128 * panel - 512, 128 * panel - 384):
                row = jnp.clip(take[j // 128, j % 128], 0, 1023)
                sketch[j : j + 1, :] = received[pl.ds(row, 1), :]

    wait_bytes(gram.at[pl.ds(0, 127)], sum_sem.at[3])
    factor(gram[...], upper_ref, inverse, work, take_rows)

    for part in range(8):
        core_copy(part).wait_send()
    for part in range(16):
        for stage in range(1, 7):
            link_copy(part, stage).wait_send()
    wait_bytes(outgoing.at[pl.ds(0, 1016)], row_sem.at[0])
    wait_bytes(gram_part.at[pl.ds(0, 127)], sum_sem.at[0])
    wait_bytes(gram_part.at[pl.ds(0, 127)], sum_sem.at[2])


def finish(sketch_ref, inverse_ref, factor_ref, q_ref, upper_ref):
    upper_ref[...] = factor_ref[...]
    q_ref[...] = dot_exact(sketch_ref[...], inverse_ref[...], ((1,), (1,)))


def per_device(features, sign_bits, sample_device, sample_offset):
    f32, i32 = jnp.float32, jnp.int32
    dma = pltpu.SemaphoreType.DMA
    sketch, inverse, upper = pl.pallas_call(
        kernel,
        out_shape=[
            jax.ShapeDtypeStruct((512, 128), f32),
            jax.ShapeDtypeStruct((128, 128), f32),
            jax.ShapeDtypeStruct((128, 128), f32),
        ],
        in_specs=[pl.BlockSpec(memory_space=pltpu.HBM)] * 4,
        out_specs=[pl.BlockSpec(memory_space=pltpu.VMEM)] * 3,
        scratch_shapes=[
            pltpu.VMEM((64, 128), i32),
            pltpu.VMEM((512, 128), i32),
            pltpu.VMEM((512, 128), i32),
            pltpu.VMEM((8192, 128), f32),
            pltpu.VMEM((128, 128), f32),
            pltpu.VMEM((8, 64, 8, 128), f32),
            pltpu.VMEM((8, 64, 8, 128), f32),
            pltpu.VMEM((8, 64, 8, 128), f32),
            pltpu.VMEM((16, 6, 32, 8, 128), f32),
            pltpu.VMEM((16, 2, 32, 8, 128), f32),
            pltpu.VMEM((16, 6, 32, 8, 128), f32),
            pltpu.VMEM((8200, 128), f32),
            pltpu.VMEM((8, 128), i32),
            pltpu.VMEM((8, 128), i32),
            pltpu.SMEM((8, 128), i32),
            pltpu.SMEM((8, 128), i32),
            pltpu.VMEM((1024, 128), f32),
            pltpu.VMEM((1024, 128), f32),
            pltpu.VMEM((128, 128), f32),
            pltpu.VMEM((128, 128), f32),
            pltpu.VMEM((1, 128), f32),
            pltpu.VMEM((128, 128), f32),
            pltpu.VMEM((128, 256), f32),
            dma((11,)),
            dma((2,)),
            dma((8,)),
            dma((8,)),
            dma((16, 6)),
            dma((16, 6)),
            dma((2,)),
            dma((4,)),
        ],
        compiler_params=pltpu.CompilerParams(
            collective_id=0, has_side_effects=True, vmem_limit_bytes=50 * 2**20
        ),
    )(
        features,
        *[pltpu.with_memory_space_constraint(a, pltpu.HBM) for a in (sign_bits.reshape(64, 128), sample_device.reshape(512, 128), sample_offset.reshape(512, 128))],
    )
    return pl.pallas_call(
        finish,
        out_shape=[
            jax.ShapeDtypeStruct((512, 128), f32),
            jax.ShapeDtypeStruct((128, 128), f32),
        ],
        compiler_params=pltpu.CompilerParams(vmem_limit_bytes=8 * 2**20),
    )(sketch, inverse, upper)


def solution(mesh):
    placed = (P(("exa", "exb"), None), P(("exa", "exb")), P(), P())
    return jax.shard_map(
        per_device,
        mesh=mesh,
        in_specs=placed,
        out_specs=(P(("exa", "exb"), None), P()),
        check_vma=False,
    )
```

```python
import jax
import jax.numpy as jnp
from jax import lax
from jax.experimental import pallas as pl
from jax.experimental.pallas import tpu as pltpu
from jax.sharding import PartitionSpec as P

MESH = pl.DeviceIdType.MESH
GROUP_BITS = (6, 5, 3, 2, 1, 0)
STEPS = (96, 32, 12, 4, 3, 1)
CORE_BIT = 4
FIRST = (0, 3, 1, 4, 2, 5, 0, 3, 1, 4, 2, 5, 0, 3, 1, 4)
ORDER = (
    (0, 0), (1, 0), (2, 0), (3, 0), (4, 0), (5, 0), (6, 0), (7, 0), (0, 1), (1, 1),
    (2, 1), (3, 1), (4, 1), (5, 1), (6, 1), (7, 1), (8, 1), (9, 1), (10, 1), (11, 1),
    (12, 1), (13, 1), (14, 1), (15, 1), (2, 2), (3, 2), (5, 2), (4, 2), (0, 2), (1, 2),
    (8, 2), (9, 2), (11, 2), (10, 2), (6, 2), (7, 2), (14, 2), (15, 2), (3, 3), (2, 3),
    (12, 2), (13, 2), (0, 3), (1, 3), (9, 3), (8, 3), (5, 3), (4, 3), (6, 3), (7, 3),
    (15, 3), (14, 3), (11, 3), (10, 3), (12, 3), (13, 3), (1, 4), (0, 4), (3, 4), (2, 4),
    (5, 4), (4, 4), (7, 4), (6, 4), (9, 4), (8, 4), (11, 4), (10, 4), (13, 4), (12, 4),
    (15, 4), (14, 4), (3, 5), (2, 5), (4, 5), (5, 5), (1, 5), (0, 5), (9, 5), (8, 5),
    (10, 5), (11, 5), (7, 5), (6, 5), (15, 5), (14, 5), (2, 6), (3, 6), (13, 5), (12, 5),
    (1, 6), (0, 6), (8, 6), (9, 6), (4, 6), (5, 6), (7, 6), (6, 6), (14, 6), (15, 6),
    (10, 6), (11, 6), (13, 6), (12, 6),
)
SCALE = 1.0 / 1024.0


def bit_of(number, bit):
    return (number // (1 << bit)) % 2


def flip(number, mask):
    for bit in range(7):
        if mask >> bit & 1:
            number = number + (1 << bit) * (1 - 2 * bit_of(number, bit))
    return number


def group_of(device):
    out = 0
    for bit in range(7):
        value = bit_of(device, bit)
        if bit in (0, 2, 5):
            above = bit_of(device, bit + 1)
            value = value + above - 2 * value * above
        out = out + value * (1 << bit)
    return out


def place_of(device):
    return (device // 16, device % 16)


def sublane_hadamard(tile, rows):
    for step in (4, 2, 1):
        high = (rows // step) % 2 == 1
        if step == 4:
            other = pltpu.roll(tile, 4, 0)
        else:
            other = jnp.where(high, pltpu.roll(tile, step, 0), pltpu.roll(tile, 8 - step, 0))
        tile = jnp.where(high, other - tile, tile + other)
    return tile


def factor(gram, upper_ref, inverse_ref, work, beside):
    width, size = 128, 16
    rows = lax.broadcasted_iota(jnp.int32, (8, width), 0)
    lanes = lax.broadcasted_iota(jnp.int32, (8, width), 1)
    work[:, :width] = gram
    work[:, width:] = (
        lax.broadcasted_iota(jnp.int32, (width, width), 0)
        == lax.broadcasted_iota(jnp.int32, (width, width), 1)
    ).astype(jnp.float32)
    both = work[:size, :]
    for panel in range(width // size):
        beside(panel)
        low, end = size * panel, size * (panel + 1)
        left = [both[8 * t : 8 * t + 8, :width] for t in range(2)]
        right = [both[8 * t : 8 * t + 8, width:] for t in range(2)]
        cols = [
            [jnp.broadcast_to(tile[:, low + j : low + j + 1], (8, width)) for tile in left]
            for j in range(size)
        ]
        pivots = [jnp.ones((8, width), jnp.float32) for _ in range(2)]
        for i in range(size):
            own, row = divmod(i, 8)
            pivot = jnp.broadcast_to(cols[i][own][row : row + 1, :], (8, width))
            pivots[own] = jnp.where(rows == row, pivot, pivots[own])
            left_row, right_row = left[own][row : row + 1, :], right[own][row : row + 1, :]
            col_row = [cols[j][own][row : row + 1, :] for j in range(size)]
            for t in range(own, 2):
                if t == own and row == 7:
                    continue
                scaled = cols[i][t] / pivot
                if t == own:
                    scaled = jnp.where(rows > row, scaled, 0.0)
                for j in range(i + 1, size):
                    cols[j][t] = cols[j][t] - scaled * col_row[j]
                left[t] = left[t] - scaled * left_row
                right[t] = right[t] - scaled * right_row
        for t in range(2):
            root = lax.rsqrt(pivots[t])
            root = root * (1.5 - 0.5 * pivots[t] * root * root)
            left[t] = jnp.where(lanes >= rows + (low + 8 * t), left[t] * root, 0.0)
            right[t] = right[t] * root
            upper_ref[low + 8 * t : low + 8 * t + 8, :] = left[t]
            inverse_ref[low + 8 * t : low + 8 * t + 8, :] = right[t]
        if end < width:
            top = jnp.concatenate(left, axis=0)
            turned = top.T
            top = jnp.concatenate([top, jnp.concatenate(right, axis=0)], axis=1)
            both = work[end : end + size, :] - dot_exact(turned[end : end + size, :], top, ((1,), (0,)))
            if end + size < width:
                work[end + size :, :] = work[end + size :, :] - dot_exact(
                    turned[end + size :, :], top, ((1,), (0,))
                )


def dot_exact(a, b, contract):
    return lax.dot_general(
        a,
        b,
        (contract, ((), ())),
        precision=lax.Precision.HIGHEST,
        preferred_element_type=jnp.float32,
    )


def sample_tables(group, device, device_ref, offset_ref, give_ref, take_ref):
    shape = (512, 128)
    offsets = offset_ref[...]
    sources = device_ref[...]
    here = offsets // 64 == group
    mine = jnp.where(here, 1.0, 0.0)
    square = (128, 128)
    first = lax.broadcasted_iota(jnp.int32, square, 0)
    second = lax.broadcasted_iota(jnp.int32, square, 1)
    before = jnp.where(first < second, 1.0, 0.0).astype(jnp.bfloat16)
    ones = jnp.ones(square, jnp.bfloat16)

    def plain(a, b):
        return lax.dot_general(
            a.astype(jnp.bfloat16),
            b.astype(jnp.bfloat16),
            (((1,), (0,)), ((), ())),
            preferred_element_type=jnp.float32,
        )

    wide = (512, 512)
    later = lax.broadcasted_iota(jnp.int32, wide, 0)
    earlier = lax.broadcasted_iota(jnp.int32, wide, 1)
    lines = jnp.where((later // 4 == earlier // 4) & (earlier < later), 1.0, 0.0)
    rank = plain(mine, before) + plain(lines, plain(mine, ones))
    value = (sources * 8192 + offsets + 1).astype(jnp.float32)
    lanes = lax.broadcasted_iota(jnp.int32, shape, 1)
    found = jnp.zeros(shape, jnp.float32)
    for k in range(8):
        chosen = jnp.where(here & (rank == float(k)), value, 0.0)
        found = jnp.where(lanes == k, jnp.sum(chosen, axis=1, keepdims=True), found)
    blocks = jnp.where(
        lax.broadcasted_iota(jnp.int32, shape, 0) // 4
        == lax.broadcasted_iota(jnp.int32, shape, 1),
        1.0,
        0.0,
    )
    slots = dot_exact(found, blocks, ((0,), (0,)))[0:8, :].astype(jnp.int32)
    full = slots - 1
    source = full // 8192
    offset = full % 8192
    natural = jnp.zeros_like(full)
    for link in range(6):
        step = STEPS[link]
        sign = jnp.zeros_like(full)
        for bit in range(7):
            if step >> bit & 1:
                sign = sign + (source // (1 << bit)) % 2
        natural = natural + (sign % 2) * (1 << (5 - link))
    part = 2 * ((offset // 8) % 8) + (source // (1 << CORE_BIT)) % 2
    spot = jnp.zeros_like(full)
    for number in range(16):
        turn = FIRST[number]
        turned = (natural % (1 << (6 - turn))) * (1 << turn) + natural // (1 << (6 - turn))
        spot = jnp.where(part == number, turned, spot)
    row = part * 512 + spot * 8 + offset % 8
    give_ref[...] = jnp.clip(jnp.where(slots > 0, row, 8192), 0, 8192)

    total = jnp.zeros(square, jnp.float32)
    for q in range(4):
        groups = offset_ref[pl.ds(4 * device + q, 1), :] // 64
        same = jnp.where(groups == first, 1.0, 0.0)
        count = plain(same, before) + total
        place = jnp.sum(same * count, axis=0, keepdims=True)
        take_ref[q : q + 1, :] = jnp.clip(groups * 8 + place.astype(jnp.int32), 0, 1023)
        total = total + plain(same, ones)


def kernel(
    features_ref,
    bits_hbm,
    device_hbm,
    offset_hbm,
    sketch,
    inverse,
    upper_ref,
    bits_ref,
    device_ref,
    offset_ref,
    rows_in,
    signs,
    core_send,
    core_keep,
    core_got,
    send,
    keep,
    got,
    held,
    give_v,
    take_v,
    give,
    take,
    outgoing,
    received,
    gram_part,
    gram_got,
    gram_row,
    gram,
    work,
    in_sem,
    table_sem,
    core_send_sem,
    core_got_sem,
    send_sem,
    got_sem,
    row_sem,
    sum_sem,
):
    device = lax.axis_index("exa") * 16 + lax.axis_index("exb")
    group = group_of(device)
    partners = [flip(device, 1 << CORE_BIT)] + [flip(device, step) for step in STEPS]
    core_sign = (1 - 2 * bit_of(group, CORE_BIT)).astype(jnp.float32)
    link_sign = [(1 - 2 * bit_of(group, bit)).astype(jnp.float32) for bit in GROUP_BITS]

    loads = [
        pltpu.make_async_copy(
            features_ref.at[pl.ds(1024 * c, 1024)], rows_in.at[pl.ds(1024 * c, 1024)], in_sem.at[c]
        )
        for c in range(8)
    ]
    small = [
        pltpu.make_async_copy(bits_hbm, bits_ref, in_sem.at[8]),
        pltpu.make_async_copy(device_hbm, device_ref, in_sem.at[9]),
        pltpu.make_async_copy(offset_hbm, offset_ref, in_sem.at[10]),
    ]
    small[0].start()
    for load in loads:
        load.start()
    small[1].start()
    small[2].start()
    barrier = pltpu.get_barrier_semaphore()
    for partner in partners:
        pl.semaphore_signal(barrier, inc=1, device_id=place_of(partner), device_id_type=MESH)

    small[0].wait()
    bits = (2 * bits_ref[...] - 1).astype(jnp.float32)
    signs[...] = jnp.transpose(jnp.concatenate([bits, bits], axis=0))

    def first_pass(pair):
        def body(low, carry):
            turned = signs[...]
            for half in range(2):
                tiles = []
                for side in range(2):
                    base = pl.multiple_of(2048 * pair + 1024 * side + 128 * low + 64 * half, 64)
                    column = 0
                    some = []
                    for t in range(8):
                        sign = jnp.broadcast_to(
                            turned[64 * half + 8 * t : 64 * half + 8 * t + 8, 8 * side : 8 * side + 1], (8, 128)
                        )
                        some.append(rows_in[pl.ds(pl.multiple_of(base + 8 * t, 8), 8), :] * sign)
                    for step in (1, 2, 4):
                        for t in range(8):
                            if not t & step:
                                a, b = some[t], some[t + step]
                                some[t], some[t + step] = a + b, a - b
                    tiles.append(some)
                spot = 16 * pair + 2 * low + half
                for t in range(8):
                    a, b = tiles[0][t], core_sign * tiles[1][t]
                    core_keep[t, spot] = a + b
                    core_send[t, spot] = a - b
            signs[...] = pltpu.roll(turned, 127, 1)
            return carry

        lax.fori_loop(0, 8, body, 0)

    def core_copy(part):
        return pltpu.make_async_remote_copy(
            src_ref=core_send.at[part],
            dst_ref=core_got.at[part],
            send_sem=core_send_sem.at[part],
            recv_sem=core_got_sem.at[part],
            device_id=place_of(partners[0]),
            device_id_type=MESH,
        )

    for pair in range(4):
        loads[2 * pair].wait()
        loads[2 * pair + 1].wait()
        first_pass(pair)
        if pair < 3:
            signs[...] = pltpu.roll(signs[...], 120, 1)
    pl.semaphore_wait(barrier, 7)
    for part in range(8):
        core_copy(part).start()

    def link_copy(part, stage):
        link = (FIRST[part] + stage - 1) % 6
        return pltpu.make_async_remote_copy(
            src_ref=send.at[part, stage - 1],
            dst_ref=got.at[part, stage - 1],
            send_sem=send_sem.at[part, stage - 1],
            recv_sem=got_sem.at[part, stage - 1],
            device_id=place_of(partners[1 + link]),
            device_id_type=MESH,
        )

    give_copy = pltpu.make_async_copy(give_v, give, table_sem.at[0])
    take_copy = pltpu.make_async_copy(take_v, take, table_sem.at[1])

    lines = lax.broadcasted_iota(jnp.int32, (8, 128), 0)

    def core_stage(part, side):
        number = 2 * part + side
        turn = FIRST[number]
        sign = link_sign[turn]

        def one(rot):
            spot = rot // (1 << turn) + (rot % (1 << turn)) * (1 << (6 - turn))
            a, b = core_keep[part, spot], core_got[part, spot]
            return a + b if side == 0 else core_sign * (a - b)

        def body(step, carry):
            for more in range(4):
                j = 4 * step + more
                a, b = one(j), sign * one(j + 32)
                keep[number, 0, j] = a + b
                send[number, 0, j] = a - b
            return carry

        lax.fori_loop(0, 8, body, 0)

    def link_stage(part, stage):
        link = (FIRST[part] + stage - 1) % 6
        sign, after = link_sign[link], link_sign[(link + 1) % 6]
        old, new = (stage - 1) % 2, stage % 2

        def pair(i):
            a, b = keep[part, old, i], got[part, stage - 1, i]
            return a + b, sign * (a - b)

        def body(step, carry):
            for more in range(4):
                i = 4 * step + more
                for side, (a, b) in enumerate(zip(pair(i), pair(i + 16))):
                    if stage == 2:
                        a, b = sublane_hadamard(a, lines), sublane_hadamard(b, lines)
                    b = after * b
                    keep[part, new, 2 * i + side] = a + b
                    send[part, stage, 2 * i + side] = a - b
            return carry

        lax.fori_loop(0, 4, body, 0)

    def last_stage(part):
        sign = link_sign[(FIRST[part] + 5) % 6] * SCALE

        def body(step, carry):
            for more in range(4):
                i = 4 * step + more
                a, b = keep[part, 1, i], got[part, 5, i]
                base = pl.multiple_of(512 * part + 16 * i, 16)
                held[pl.ds(base, 8), :] = SCALE * (a + b)
                held[pl.ds(pl.multiple_of(base + 8, 8), 8), :] = sign * (a - b)
            return carry

        lax.fori_loop(0, 8, body, 0)

    for number, (part, stage) in enumerate(ORDER):
        if stage == 0:
            core_copy(part).wait_recv()
            for side in range(2):
                core_stage(part, side)
                link_copy(2 * part + side, 1).start()
        else:
            link_copy(part, stage).wait_recv()
            if stage < 6:
                link_stage(part, stage)
                link_copy(part, stage + 1).start()
            else:
                last_stage(part)
        if number == 7:
            small[1].wait()
            small[2].wait()
            sample_tables(group, device, device_ref, offset_ref, give_v, take_v)
            give_copy.start()
            take_copy.start()
    held[8192:8200, :] = jnp.zeros((8, 128), jnp.float32)
    give_copy.wait()
    take_copy.wait()

    def gather(step, carry):
        for more in range(4):
            to = 4 * step + more
            for k in range(8):
                row = give[k, to]
                outgoing[pl.ds(8 * to + k, 1), :] = held[pl.ds(row, 1), :]
        return carry

    lax.fori_loop(0, 32, gather, 0)

    def row_copy(to):
        return pltpu.make_async_remote_copy(
            src_ref=outgoing.at[pl.ds(pl.multiple_of(8 * to, 8), 8)],
            dst_ref=received.at[pl.ds(pl.multiple_of(8 * group, 8), 8)],
            send_sem=row_sem.at[0],
            recv_sem=row_sem.at[1],
            device_id=place_of(to),
            device_id_type=MESH,
        )

    gram_part[...] = dot_exact(outgoing[...], outgoing[...], ((0,), (0,)))

    def part_copy(to):
        return pltpu.make_async_remote_copy(
            src_ref=gram_part.at[pl.ds(to, 1)],
            dst_ref=gram_got.at[pl.ds(device, 1)],
            send_sem=sum_sem.at[0],
            recv_sem=sum_sem.at[1],
            device_id=place_of(to),
            device_id_type=MESH,
        )

    def sum_copy(to):
        return pltpu.make_async_remote_copy(
            src_ref=gram_row,
            dst_ref=gram.at[pl.ds(device, 1)],
            send_sem=sum_sem.at[2],
            recv_sem=sum_sem.at[3],
            device_id=place_of(to),
            device_id_type=MESH,
        )

    exa, exb = lax.axis_index("exa"), lax.axis_index("exb")
    turns = (2, 3, 1, 0)
    lower = {dz: 32 * ((exa // 2 + dz) % 4) for dz in turns}
    middle = {dx: 4 * ((exb // 4 + dx) % 4) for dx in turns}
    upper = {dy: (exb + dy) % 4 for dy in turns}
    cores = (16 * (1 - exa % 2), 16 * (exa % 2))
    shifts = [(z, x, y, c) for z in turns for x in turns for y in turns for c in (0, 1)]
    shifts = sorted(shifts, key=lambda t: -sum(min(v, 4 - v) for v in t[:3]))

    def all_others(copy):
        for z, x, y, c in shifts[:-1]:
            copy(lower[z] + cores[c] + (middle[x] + upper[y])).start()

    def wait_bytes(ref, sem):
        pltpu.make_async_copy(ref, ref, sem).wait()

    all_others(part_copy)
    gram_got[pl.ds(device, 1), :] = gram_part[pl.ds(device, 1), :]
    wait_bytes(gram_got.at[pl.ds(0, 127)], sum_sem.at[1])
    gram_row[...] = jnp.sum(gram_got[...], axis=0, keepdims=True) * (1.0 / 65536.0)
    all_others(sum_copy)
    gram[pl.ds(device, 1), :] = gram_row[...]
    all_others(row_copy)
    received[pl.ds(pl.multiple_of(8 * group, 8), 8), :] = outgoing[
        pl.ds(pl.multiple_of(8 * device, 8), 8), :
    ]

    def take_rows(panel):
        if panel == 6:
            wait_bytes(received.at[pl.ds(0, 1016)], row_sem.at[1])
        if panel >= 6:
            for j in range(256 * (panel - 6), 256 * (panel - 5)):
                row = take[j // 128, j % 128]
                sketch[j : j + 1, :] = received[pl.ds(row, 1), :]

    wait_bytes(gram.at[pl.ds(0, 127)], sum_sem.at[3])
    factor(gram[...], upper_ref, inverse, work, take_rows)

    for part in range(8):
        core_copy(part).wait_send()
    for part in range(16):
        for stage in range(1, 7):
            link_copy(part, stage).wait_send()
    wait_bytes(outgoing.at[pl.ds(0, 1016)], row_sem.at[0])
    wait_bytes(gram_part.at[pl.ds(0, 127)], sum_sem.at[0])
    wait_bytes(gram_part.at[pl.ds(0, 127)], sum_sem.at[2])


def finish(sketch_ref, inverse_ref, factor_ref, q_ref, upper_ref):
    upper_ref[...] = factor_ref[...]
    q_ref[...] = dot_exact(sketch_ref[...], inverse_ref[...], ((1,), (1,)))


def per_device(features, sign_bits, sample_device, sample_offset):
    f32, i32 = jnp.float32, jnp.int32
    dma = pltpu.SemaphoreType.DMA
    sketch, inverse, upper = pl.pallas_call(
        kernel,
        out_shape=[
            jax.ShapeDtypeStruct((512, 128), f32),
            jax.ShapeDtypeStruct((128, 128), f32),
            jax.ShapeDtypeStruct((128, 128), f32),
        ],
        in_specs=[pl.BlockSpec(memory_space=pltpu.HBM)] * 4,
        out_specs=[pl.BlockSpec(memory_space=pltpu.VMEM)] * 3,
        scratch_shapes=[
            pltpu.VMEM((64, 128), i32),
            pltpu.VMEM((512, 128), i32),
            pltpu.VMEM((512, 128), i32),
            pltpu.VMEM((8192, 128), f32),
            pltpu.VMEM((128, 128), f32),
            pltpu.VMEM((8, 64, 8, 128), f32),
            pltpu.VMEM((8, 64, 8, 128), f32),
            pltpu.VMEM((8, 64, 8, 128), f32),
            pltpu.VMEM((16, 6, 32, 8, 128), f32),
            pltpu.VMEM((16, 2, 32, 8, 128), f32),
            pltpu.VMEM((16, 6, 32, 8, 128), f32),
            pltpu.VMEM((8200, 128), f32),
            pltpu.VMEM((8, 128), i32),
            pltpu.VMEM((8, 128), i32),
            pltpu.SMEM((8, 128), i32),
            pltpu.SMEM((8, 128), i32),
            pltpu.VMEM((1024, 128), f32),
            pltpu.VMEM((1024, 128), f32),
            pltpu.VMEM((128, 128), f32),
            pltpu.VMEM((128, 128), f32),
            pltpu.VMEM((1, 128), f32),
            pltpu.VMEM((128, 128), f32),
            pltpu.VMEM((128, 256), f32),
            dma((11,)),
            dma((2,)),
            dma((8,)),
            dma((8,)),
            dma((16, 6)),
            dma((16, 6)),
            dma((2,)),
            dma((4,)),
        ],
        compiler_params=pltpu.CompilerParams(
            collective_id=0, has_side_effects=True, vmem_limit_bytes=50 * 2**20
        ),
    )(
        features,
        *[pltpu.with_memory_space_constraint(a, pltpu.HBM) for a in (sign_bits.reshape(64, 128), sample_device.reshape(512, 128), sample_offset.reshape(512, 128))],
    )
    return pl.pallas_call(
        finish,
        out_shape=[
            jax.ShapeDtypeStruct((512, 128), f32),
            jax.ShapeDtypeStruct((128, 128), f32),
        ],
        compiler_params=pltpu.CompilerParams(vmem_limit_bytes=8 * 2**20),
    )(sketch, inverse, upper)


def solution(mesh):
    placed = (P(("exa", "exb"), None), P(("exa", "exb")), P(), P())
    return jax.shard_map(
        per_device,
        mesh=mesh,
        in_specs=placed,
        out_specs=(P(("exa", "exb"), None), P()),
        check_vma=False,
    )
```

```python
import jax
import jax.numpy as jnp
from jax import lax
from jax.experimental import pallas as pl
from jax.experimental.pallas import tpu as pltpu
from jax.sharding import PartitionSpec as P

MESH = pl.DeviceIdType.MESH
GROUP_BITS = (6, 5, 3, 2, 1, 0)
STEPS = (96, 32, 12, 4, 3, 1)
CORE_BIT = 4
FIRST = (0, 2, 4, 1, 3, 5, 0, 2, 4, 1, 3, 5, 0, 2, 4, 1)
ORDER = (
    (0, 0), (1, 0), (2, 0), (3, 0), (4, 0), (5, 0), (6, 0), (7, 0), (0, 1), (1, 1),
    (2, 1), (3, 1), (4, 1), (5, 1), (6, 1), (7, 1), (8, 1), (9, 1), (10, 1), (11, 1),
    (12, 1), (13, 1), (14, 1), (15, 1), (1, 2), (2, 2), (5, 2), (3, 2), (4, 2), (0, 2),
    (7, 2), (8, 2), (11, 2), (9, 2), (10, 2), (6, 2), (13, 2), (14, 2), (2, 3), (15, 2),
    (1, 3), (12, 2), (3, 3), (4, 3), (8, 3), (0, 3), (7, 3), (5, 3), (9, 3), (10, 3),
    (14, 3), (6, 3), (13, 3), (11, 3), (15, 3), (1, 4), (4, 4), (12, 3), (3, 4), (2, 4),
    (0, 4), (7, 4), (10, 4), (5, 4), (9, 4), (8, 4), (6, 4), (13, 4), (1, 5), (11, 4),
    (15, 4), (14, 4), (12, 4), (3, 5), (7, 5), (2, 5), (0, 5), (4, 5), (5, 5), (9, 5),
    (13, 5), (8, 5), (6, 5), (10, 5), (11, 5), (15, 5), (3, 6), (14, 5), (12, 5), (1, 6),
    (2, 6), (0, 6), (9, 6), (4, 6), (5, 6), (7, 6), (8, 6), (6, 6), (15, 6), (10, 6),
    (11, 6), (13, 6), (14, 6), (12, 6),
)
SCALE = 1.0 / 1024.0


def bit_of(number, bit):
    return (number // (1 << bit)) % 2


def flip(number, mask):
    for bit in range(7):
        if mask >> bit & 1:
            number = number + (1 << bit) * (1 - 2 * bit_of(number, bit))
    return number


def group_of(device):
    out = 0
    for bit in range(7):
        value = bit_of(device, bit)
        if bit in (0, 2, 5):
            above = bit_of(device, bit + 1)
            value = value + above - 2 * value * above
        out = out + value * (1 << bit)
    return out


def place_of(device):
    return (device // 16, device % 16)


def sublane_hadamard(tile, rows):
    for step in (4, 2, 1):
        high = (rows // step) % 2 == 1
        if step == 4:
            other = pltpu.roll(tile, 4, 0)
        else:
            other = jnp.where(high, pltpu.roll(tile, step, 0), pltpu.roll(tile, 8 - step, 0))
        tile = jnp.where(high, other - tile, tile + other)
    return tile


def factor(gram, upper_ref, inverse_ref, work, beside):
    width, size = 128, 16
    rows = lax.broadcasted_iota(jnp.int32, (8, width), 0)
    lanes = lax.broadcasted_iota(jnp.int32, (8, width), 1)
    work[:, :width] = gram
    work[:, width:] = (
        lax.broadcasted_iota(jnp.int32, (width, width), 0)
        == lax.broadcasted_iota(jnp.int32, (width, width), 1)
    ).astype(jnp.float32)
    both = work[:size, :]
    for panel in range(width // size):
        beside(panel)
        low, end = size * panel, size * (panel + 1)
        left = [both[8 * t : 8 * t + 8, :width] for t in range(2)]
        right = [both[8 * t : 8 * t + 8, width:] for t in range(2)]
        cols = [
            [jnp.broadcast_to(tile[:, low + j : low + j + 1], (8, width)) for tile in left]
            for j in range(size)
        ]
        pivots = [jnp.ones((8, width), jnp.float32) for _ in range(2)]
        for i in range(size):
            own, row = divmod(i, 8)
            pivot = jnp.broadcast_to(cols[i][own][row : row + 1, :], (8, width))
            pivots[own] = jnp.where(rows == row, pivot, pivots[own])
            left_row, right_row = left[own][row : row + 1, :], right[own][row : row + 1, :]
            col_row = [cols[j][own][row : row + 1, :] for j in range(size)]
            for t in range(own, 2):
                if t == own and row == 7:
                    continue
                scaled = cols[i][t] / pivot
                if t == own:
                    scaled = jnp.where(rows > row, scaled, 0.0)
                for j in range(i + 1, size):
                    cols[j][t] = cols[j][t] - scaled * col_row[j]
                left[t] = left[t] - scaled * left_row
                right[t] = right[t] - scaled * right_row
        for t in range(2):
            root = lax.rsqrt(pivots[t])
            root = root * (1.5 - 0.5 * pivots[t] * root * root)
            left[t] = jnp.where(lanes >= rows + (low + 8 * t), left[t] * root, 0.0)
            right[t] = right[t] * root
            upper_ref[low + 8 * t : low + 8 * t + 8, :] = left[t]
            inverse_ref[low + 8 * t : low + 8 * t + 8, :] = right[t]
        if end < width:
            top = jnp.concatenate(left, axis=0)
            turned = top.T
            top = jnp.concatenate([top, jnp.concatenate(right, axis=0)], axis=1)
            both = work[end : end + size, :] - dot_exact(turned[end : end + size, :], top, ((1,), (0,)))
            if end + size < width:
                work[end + size :, :] = work[end + size :, :] - dot_exact(
                    turned[end + size :, :], top, ((1,), (0,))
                )


def dot_exact(a, b, contract):
    return lax.dot_general(
        a,
        b,
        (contract, ((), ())),
        precision=lax.Precision.HIGHEST,
        preferred_element_type=jnp.float32,
    )


def sample_tables(group, device, device_ref, offset_ref, give_ref, take_ref):
    shape = (512, 128)
    offsets = offset_ref[...]
    sources = device_ref[...]
    here = offsets // 64 == group
    mine = jnp.where(here, 1.0, 0.0)
    square = (128, 128)
    first = lax.broadcasted_iota(jnp.int32, square, 0)
    second = lax.broadcasted_iota(jnp.int32, square, 1)
    before = jnp.where(first < second, 1.0, 0.0).astype(jnp.bfloat16)
    ones = jnp.ones(square, jnp.bfloat16)

    def plain(a, b):
        return lax.dot_general(
            a.astype(jnp.bfloat16),
            b.astype(jnp.bfloat16),
            (((1,), (0,)), ((), ())),
            preferred_element_type=jnp.float32,
        )

    wide = (512, 512)
    later = lax.broadcasted_iota(jnp.int32, wide, 0)
    earlier = lax.broadcasted_iota(jnp.int32, wide, 1)
    lines = jnp.where((later // 4 == earlier // 4) & (earlier < later), 1.0, 0.0)
    rank = plain(mine, before) + plain(lines, plain(mine, ones))
    value = (sources * 8192 + offsets + 1).astype(jnp.float32)
    lanes = lax.broadcasted_iota(jnp.int32, shape, 1)
    found = jnp.zeros(shape, jnp.float32)
    for k in range(8):
        chosen = jnp.where(here & (rank == float(k)), value, 0.0)
        found = jnp.where(lanes == k, jnp.sum(chosen, axis=1, keepdims=True), found)
    blocks = jnp.where(
        lax.broadcasted_iota(jnp.int32, shape, 0) // 4
        == lax.broadcasted_iota(jnp.int32, shape, 1),
        1.0,
        0.0,
    )
    slots = dot_exact(found, blocks, ((0,), (0,)))[0:8, :].astype(jnp.int32)
    full = slots - 1
    source = full // 8192
    offset = full % 8192
    natural = jnp.zeros_like(full)
    for link in range(6):
        step = STEPS[link]
        sign = jnp.zeros_like(full)
        for bit in range(7):
            if step >> bit & 1:
                sign = sign + (source // (1 << bit)) % 2
        natural = natural + (sign % 2) * (1 << (5 - link))
    part = 2 * ((offset // 8) % 8) + (source // (1 << CORE_BIT)) % 2
    spot = jnp.zeros_like(full)
    for number in range(16):
        turn = FIRST[number]
        turned = (natural % (1 << (6 - turn))) * (1 << turn) + natural // (1 << (6 - turn))
        spot = jnp.where(part == number, turned, spot)
    row = part * 512 + spot * 8 + offset % 8
    give_ref[...] = jnp.clip(jnp.where(slots > 0, row, 8192), 0, 8192)

    total = jnp.zeros(square, jnp.float32)
    for q in range(4):
        groups = offset_ref[pl.ds(4 * device + q, 1), :] // 64
        same = jnp.where(groups == first, 1.0, 0.0)
        count = plain(same, before) + total
        place = jnp.sum(same * count, axis=0, keepdims=True)
        take_ref[q : q + 1, :] = jnp.clip(groups * 8 + place.astype(jnp.int32), 0, 1023)
        total = total + plain(same, ones)


def kernel(
    features_ref,
    bits_hbm,
    device_hbm,
    offset_hbm,
    sketch,
    inverse,
    upper_ref,
    bits_ref,
    device_ref,
    offset_ref,
    rows_in,
    signs,
    core_send,
    core_keep,
    core_got,
    send,
    keep,
    got,
    held,
    give_v,
    take_v,
    give,
    take,
    outgoing,
    received,
    gram_part,
    gram_got,
    gram_row,
    gram,
    work,
    in_sem,
    table_sem,
    core_send_sem,
    core_got_sem,
    send_sem,
    got_sem,
    row_sem,
    sum_sem,
):
    device = lax.axis_index("exa") * 16 + lax.axis_index("exb")
    group = group_of(device)
    partners = [flip(device, 1 << CORE_BIT)] + [flip(device, step) for step in STEPS]
    core_sign = (1 - 2 * bit_of(group, CORE_BIT)).astype(jnp.float32)
    link_sign = [(1 - 2 * bit_of(group, bit)).astype(jnp.float32) for bit in GROUP_BITS]

    loads = [
        pltpu.make_async_copy(
            features_ref.at[pl.ds(1024 * c, 1024)], rows_in.at[pl.ds(1024 * c, 1024)], in_sem.at[c]
        )
        for c in range(8)
    ]
    small = [
        pltpu.make_async_copy(bits_hbm, bits_ref, in_sem.at[8]),
        pltpu.make_async_copy(device_hbm, device_ref, in_sem.at[9]),
        pltpu.make_async_copy(offset_hbm, offset_ref, in_sem.at[10]),
    ]
    small[0].start()
    for load in loads:
        load.start()
    small[1].start()
    small[2].start()
    barrier = pltpu.get_barrier_semaphore()
    for partner in partners:
        pl.semaphore_signal(barrier, inc=1, device_id=place_of(partner), device_id_type=MESH)

    small[0].wait()
    bits = (2 * bits_ref[...] - 1).astype(jnp.float32)
    signs[...] = jnp.transpose(jnp.concatenate([bits, bits], axis=0))

    def first_pass(pair):
        def body(low, carry):
            turned = signs[...]
            for half in range(2):
                tiles = []
                for side in range(2):
                    base = pl.multiple_of(2048 * pair + 1024 * side + 128 * low + 64 * half, 64)
                    column = 0
                    some = []
                    for t in range(8):
                        sign = jnp.broadcast_to(
                            turned[64 * half + 8 * t : 64 * half + 8 * t + 8, 8 * side : 8 * side + 1], (8, 128)
                        )
                        some.append(rows_in[pl.ds(pl.multiple_of(base + 8 * t, 8), 8), :] * sign)
                    for step in (1, 2, 4):
                        for t in range(8):
                            if not t & step:
                                a, b = some[t], some[t + step]
                                some[t], some[t + step] = a + b, a - b
                    tiles.append(some)
                spot = 16 * pair + 2 * low + half
                for t in range(8):
                    a, b = tiles[0][t], core_sign * tiles[1][t]
                    core_keep[t, spot] = a + b
                    core_send[t, spot] = a - b
            signs[...] = pltpu.roll(turned, 127, 1)
            return carry

        lax.fori_loop(0, 8, body, 0)

    def core_copy(part):
        return pltpu.make_async_remote_copy(
            src_ref=core_send.at[part],
            dst_ref=core_got.at[part],
            send_sem=core_send_sem.at[part],
            recv_sem=core_got_sem.at[part],
            device_id=place_of(partners[0]),
            device_id_type=MESH,
        )

    for pair in range(4):
        loads[2 * pair].wait()
        loads[2 * pair + 1].wait()
        first_pass(pair)
        if pair < 3:
            signs[...] = pltpu.roll(signs[...], 120, 1)
    pl.semaphore_wait(barrier, 7)
    for part in range(8):
        core_copy(part).start()

    def link_copy(part, stage):
        link = (FIRST[part] + stage - 1) % 6
        return pltpu.make_async_remote_copy(
            src_ref=send.at[part, stage - 1],
            dst_ref=got.at[part, stage - 1],
            send_sem=send_sem.at[part, stage - 1],
            recv_sem=got_sem.at[part, stage - 1],
            device_id=place_of(partners[1 + link]),
            device_id_type=MESH,
        )

    give_copy = pltpu.make_async_copy(give_v, give, table_sem.at[0])
    take_copy = pltpu.make_async_copy(take_v, take, table_sem.at[1])

    lines = lax.broadcasted_iota(jnp.int32, (8, 128), 0)

    def core_stage(part, side):
        number = 2 * part + side
        turn = FIRST[number]
        sign = link_sign[turn]

        def one(rot):
            spot = rot // (1 << turn) + (rot % (1 << turn)) * (1 << (6 - turn))
            a, b = core_keep[part, spot], core_got[part, spot]
            return a + b if side == 0 else core_sign * (a - b)

        def body(step, carry):
            for more in range(4):
                j = 4 * step + more
                a, b = one(j), sign * one(j + 32)
                keep[number, 0, j] = a + b
                send[number, 0, j] = a - b
            return carry

        lax.fori_loop(0, 8, body, 0)

    def link_stage(part, stage):
        link = (FIRST[part] + stage - 1) % 6
        sign, after = link_sign[link], link_sign[(link + 1) % 6]
        old, new = (stage - 1) % 2, stage % 2

        def pair(i):
            a, b = keep[part, old, i], got[part, stage - 1, i]
            return a + b, sign * (a - b)

        def body(step, carry):
            for more in range(4):
                i = 4 * step + more
                for side, (a, b) in enumerate(zip(pair(i), pair(i + 16))):
                    if stage == 2:
                        a, b = sublane_hadamard(a, lines), sublane_hadamard(b, lines)
                    b = after * b
                    keep[part, new, 2 * i + side] = a + b
                    send[part, stage, 2 * i + side] = a - b
            return carry

        lax.fori_loop(0, 4, body, 0)

    def last_stage(part):
        sign = link_sign[(FIRST[part] + 5) % 6] * SCALE

        def body(step, carry):
            for more in range(4):
                i = 4 * step + more
                a, b = keep[part, 1, i], got[part, 5, i]
                base = pl.multiple_of(512 * part + 16 * i, 16)
                held[pl.ds(base, 8), :] = SCALE * (a + b)
                held[pl.ds(pl.multiple_of(base + 8, 8), 8), :] = sign * (a - b)
            return carry

        lax.fori_loop(0, 8, body, 0)

    for number, (part, stage) in enumerate(ORDER):
        if stage == 0:
            core_copy(part).wait_recv()
            for side in range(2):
                core_stage(part, side)
                link_copy(2 * part + side, 1).start()
        else:
            link_copy(part, stage).wait_recv()
            if stage < 6:
                link_stage(part, stage)
                link_copy(part, stage + 1).start()
            else:
                last_stage(part)
        if number == 7:
            small[1].wait()
            small[2].wait()
            sample_tables(group, device, device_ref, offset_ref, give_v, take_v)
            give_copy.start()
            take_copy.start()
    held[8192:8200, :] = jnp.zeros((8, 128), jnp.float32)
    give_copy.wait()
    take_copy.wait()

    def gather(step, carry):
        for more in range(4):
            to = 4 * step + more
            for k in range(8):
                row = give[k, to]
                outgoing[pl.ds(8 * to + k, 1), :] = held[pl.ds(row, 1), :]
        return carry

    lax.fori_loop(0, 32, gather, 0)

    def row_copy(to):
        return pltpu.make_async_remote_copy(
            src_ref=outgoing.at[pl.ds(pl.multiple_of(8 * to, 8), 8)],
            dst_ref=received.at[pl.ds(pl.multiple_of(8 * group, 8), 8)],
            send_sem=row_sem.at[0],
            recv_sem=row_sem.at[1],
            device_id=place_of(to),
            device_id_type=MESH,
        )

    gram_part[...] = dot_exact(outgoing[...], outgoing[...], ((0,), (0,)))

    def part_copy(to):
        return pltpu.make_async_remote_copy(
            src_ref=gram_part.at[pl.ds(to, 1)],
            dst_ref=gram_got.at[pl.ds(device, 1)],
            send_sem=sum_sem.at[0],
            recv_sem=sum_sem.at[1],
            device_id=place_of(to),
            device_id_type=MESH,
        )

    def sum_copy(to):
        return pltpu.make_async_remote_copy(
            src_ref=gram_row,
            dst_ref=gram.at[pl.ds(device, 1)],
            send_sem=sum_sem.at[2],
            recv_sem=sum_sem.at[3],
            device_id=place_of(to),
            device_id_type=MESH,
        )

    exa, exb = lax.axis_index("exa"), lax.axis_index("exb")
    turns = (2, 3, 1, 0)
    lower = {dz: 32 * ((exa // 2 + dz) % 4) for dz in turns}
    middle = {dx: 4 * ((exb // 4 + dx) % 4) for dx in turns}
    upper = {dy: (exb + dy) % 4 for dy in turns}
    cores = (16 * (1 - exa % 2), 16 * (exa % 2))
    shifts = [(z, x, y, c) for z in turns for x in turns for y in turns for c in (0, 1)]
    shifts = sorted(shifts, key=lambda t: -sum(min(v, 4 - v) for v in t[:3]))

    def all_others(copy):
        for z, x, y, c in shifts[:-1]:
            copy(lower[z] + cores[c] + (middle[x] + upper[y])).start()

    def wait_bytes(ref, sem):
        pltpu.make_async_copy(ref, ref, sem).wait()

    all_others(part_copy)
    gram_got[pl.ds(device, 1), :] = gram_part[pl.ds(device, 1), :]
    wait_bytes(gram_got.at[pl.ds(0, 127)], sum_sem.at[1])
    gram_row[...] = jnp.sum(gram_got[...], axis=0, keepdims=True) * (1.0 / 65536.0)
    all_others(sum_copy)
    gram[pl.ds(device, 1), :] = gram_row[...]
    all_others(row_copy)
    received[pl.ds(pl.multiple_of(8 * group, 8), 8), :] = outgoing[
        pl.ds(pl.multiple_of(8 * device, 8), 8), :
    ]

    def take_rows(panel):
        if panel == 6:
            wait_bytes(received.at[pl.ds(0, 1016)], row_sem.at[1])
        if panel >= 6:
            for j in range(256 * (panel - 6), 256 * (panel - 5)):
                row = take[j // 128, j % 128]
                sketch[j : j + 1, :] = received[pl.ds(row, 1), :]

    wait_bytes(gram.at[pl.ds(0, 127)], sum_sem.at[3])
    factor(gram[...], upper_ref, inverse, work, take_rows)

    for part in range(8):
        core_copy(part).wait_send()
    for part in range(16):
        for stage in range(1, 7):
            link_copy(part, stage).wait_send()
    wait_bytes(outgoing.at[pl.ds(0, 1016)], row_sem.at[0])
    wait_bytes(gram_part.at[pl.ds(0, 127)], sum_sem.at[0])
    wait_bytes(gram_part.at[pl.ds(0, 127)], sum_sem.at[2])


def finish(sketch_ref, inverse_ref, factor_ref, q_ref, upper_ref):
    upper_ref[...] = factor_ref[...]
    q_ref[...] = dot_exact(sketch_ref[...], inverse_ref[...], ((1,), (1,)))


def per_device(features, sign_bits, sample_device, sample_offset):
    f32, i32 = jnp.float32, jnp.int32
    dma = pltpu.SemaphoreType.DMA
    sketch, inverse, upper = pl.pallas_call(
        kernel,
        out_shape=[
            jax.ShapeDtypeStruct((512, 128), f32),
            jax.ShapeDtypeStruct((128, 128), f32),
            jax.ShapeDtypeStruct((128, 128), f32),
        ],
        in_specs=[pl.BlockSpec(memory_space=pltpu.HBM)] * 4,
        out_specs=[pl.BlockSpec(memory_space=pltpu.VMEM)] * 3,
        scratch_shapes=[
            pltpu.VMEM((64, 128), i32),
            pltpu.VMEM((512, 128), i32),
            pltpu.VMEM((512, 128), i32),
            pltpu.VMEM((8192, 128), f32),
            pltpu.VMEM((128, 128), f32),
            pltpu.VMEM((8, 64, 8, 128), f32),
            pltpu.VMEM((8, 64, 8, 128), f32),
            pltpu.VMEM((8, 64, 8, 128), f32),
            pltpu.VMEM((16, 6, 32, 8, 128), f32),
            pltpu.VMEM((16, 2, 32, 8, 128), f32),
            pltpu.VMEM((16, 6, 32, 8, 128), f32),
            pltpu.VMEM((8200, 128), f32),
            pltpu.VMEM((8, 128), i32),
            pltpu.VMEM((8, 128), i32),
            pltpu.SMEM((8, 128), i32),
            pltpu.SMEM((8, 128), i32),
            pltpu.VMEM((1024, 128), f32),
            pltpu.VMEM((1024, 128), f32),
            pltpu.VMEM((128, 128), f32),
            pltpu.VMEM((128, 128), f32),
            pltpu.VMEM((1, 128), f32),
            pltpu.VMEM((128, 128), f32),
            pltpu.VMEM((128, 256), f32),
            dma((11,)),
            dma((2,)),
            dma((8,)),
            dma((8,)),
            dma((16, 6)),
            dma((16, 6)),
            dma((2,)),
            dma((4,)),
        ],
        compiler_params=pltpu.CompilerParams(
            collective_id=0, has_side_effects=True, vmem_limit_bytes=50 * 2**20
        ),
    )(
        features,
        *[pltpu.with_memory_space_constraint(a, pltpu.HBM) for a in (sign_bits.reshape(64, 128), sample_device.reshape(512, 128), sample_offset.reshape(512, 128))],
    )
    return pl.pallas_call(
        finish,
        out_shape=[
            jax.ShapeDtypeStruct((512, 128), f32),
            jax.ShapeDtypeStruct((128, 128), f32),
        ],
        compiler_params=pltpu.CompilerParams(vmem_limit_bytes=8 * 2**20),
    )(sketch, inverse, upper)


def solution(mesh):
    placed = (P(("exa", "exb"), None), P(("exa", "exb")), P(), P())
    return jax.shard_map(
        per_device,
        mesh=mesh,
        in_specs=placed,
        out_specs=(P(("exa", "exb"), None), P()),
        check_vma=False,
    )
```

```python
import jax
import jax.numpy as jnp
from jax import lax
from jax.experimental import pallas as pl
from jax.experimental.pallas import tpu as pltpu
from jax.sharding import PartitionSpec as P

MESH = pl.DeviceIdType.MESH
GROUP_BITS = (6, 5, 3, 2, 1, 0)
STEPS = (96, 32, 12, 4, 3, 1)
CORE_BIT = 4
FIRST = (0, 2, 4, 1, 3, 5, 0, 2, 4, 1, 3, 5, 0, 2, 4, 1)
ORDER = (
    (0, 0), (1, 0), (2, 0), (3, 0), (4, 0), (5, 0), (6, 0), (7, 0), (0, 1), (1, 1),
    (2, 1), (3, 1), (4, 1), (5, 1), (6, 1), (7, 1), (8, 1), (9, 1), (10, 1), (11, 1),
    (12, 1), (13, 1), (14, 1), (15, 1), (1, 2), (2, 2), (5, 2), (3, 2), (4, 2), (0, 2),
    (7, 2), (8, 2), (11, 2), (9, 2), (10, 2), (6, 2), (13, 2), (14, 2), (2, 3), (15, 2),
    (1, 3), (12, 2), (3, 3), (4, 3), (8, 3), (0, 3), (7, 3), (5, 3), (9, 3), (10, 3),
    (14, 3), (6, 3), (13, 3), (11, 3), (15, 3), (1, 4), (4, 4), (12, 3), (3, 4), (2, 4),
    (0, 4), (7, 4), (10, 4), (5, 4), (9, 4), (8, 4), (6, 4), (13, 4), (1, 5), (11, 4),
    (15, 4), (14, 4), (12, 4), (3, 5), (7, 5), (2, 5), (0, 5), (4, 5), (5, 5), (9, 5),
    (13, 5), (8, 5), (6, 5), (10, 5), (11, 5), (15, 5), (3, 6), (14, 5), (12, 5), (1, 6),
    (2, 6), (0, 6), (9, 6), (4, 6), (5, 6), (7, 6), (8, 6), (6, 6), (15, 6), (10, 6),
    (11, 6), (13, 6), (14, 6), (12, 6),
)
SCALE = 1.0 / 1024.0


def bit_of(number, bit):
    return (number // (1 << bit)) % 2


def flip(number, mask):
    for bit in range(7):
        if mask >> bit & 1:
            number = number + (1 << bit) * (1 - 2 * bit_of(number, bit))
    return number


def group_of(device):
    out = 0
    for bit in range(7):
        value = bit_of(device, bit)
        if bit in (0, 2, 5):
            above = bit_of(device, bit + 1)
            value = value + above - 2 * value * above
        out = out + value * (1 << bit)
    return out


def place_of(device):
    return (device // 16, device % 16)


def sublane_hadamard(tile, rows):
    for step in (4, 2, 1):
        high = (rows // step) % 2 == 1
        if step == 4:
            other = pltpu.roll(tile, 4, 0)
        else:
            other = jnp.where(high, pltpu.roll(tile, step, 0), pltpu.roll(tile, 8 - step, 0))
        tile = jnp.where(high, other - tile, tile + other)
    return tile


def factor(gram, upper_ref, inverse_ref, work, beside):
    width, size = 128, 16
    rows = lax.broadcasted_iota(jnp.int32, (8, width), 0)
    lanes = lax.broadcasted_iota(jnp.int32, (8, width), 1)
    work[:, :width] = gram
    work[:, width:] = (
        lax.broadcasted_iota(jnp.int32, (width, width), 0)
        == lax.broadcasted_iota(jnp.int32, (width, width), 1)
    ).astype(jnp.float32)
    both = work[:size, :]
    for panel in range(width // size):
        beside(panel)
        low, end = size * panel, size * (panel + 1)
        left = [both[8 * t : 8 * t + 8, :width] for t in range(2)]
        right = [both[8 * t : 8 * t + 8, width:] for t in range(2)]
        cols = [
            [jnp.broadcast_to(tile[:, low + j : low + j + 1], (8, width)) for tile in left]
            for j in range(size)
        ]
        pivots = [jnp.ones((8, width), jnp.float32) for _ in range(2)]
        for i in range(size):
            own, row = divmod(i, 8)
            pivot = jnp.broadcast_to(cols[i][own][row : row + 1, :], (8, width))
            pivots[own] = jnp.where(rows == row, pivot, pivots[own])
            left_row, right_row = left[own][row : row + 1, :], right[own][row : row + 1, :]
            col_row = [cols[j][own][row : row + 1, :] for j in range(size)]
            for t in range(own, 2):
                if t == own and row == 7:
                    continue
                scaled = cols[i][t] / pivot
                if t == own:
                    scaled = jnp.where(rows > row, scaled, 0.0)
                for j in range(i + 1, size):
                    cols[j][t] = cols[j][t] - scaled * col_row[j]
                left[t] = left[t] - scaled * left_row
                right[t] = right[t] - scaled * right_row
        for t in range(2):
            root = lax.rsqrt(pivots[t])
            root = root * (1.5 - 0.5 * pivots[t] * root * root)
            left[t] = jnp.where(lanes >= rows + (low + 8 * t), left[t] * root, 0.0)
            right[t] = right[t] * root
            upper_ref[low + 8 * t : low + 8 * t + 8, :] = left[t]
            inverse_ref[low + 8 * t : low + 8 * t + 8, :] = right[t]
        if end < width:
            top = jnp.concatenate(left, axis=0)
            turned = top.T
            top = jnp.concatenate([top, jnp.concatenate(right, axis=0)], axis=1)
            both = work[end : end + size, :] - dot_exact(turned[end : end + size, :], top, ((1,), (0,)))
            if end + size < width:
                work[end + size :, :] = work[end + size :, :] - dot_exact(
                    turned[end + size :, :], top, ((1,), (0,))
                )


def dot_exact(a, b, contract):
    return lax.dot_general(
        a,
        b,
        (contract, ((), ())),
        precision=lax.Precision.HIGHEST,
        preferred_element_type=jnp.float32,
    )


def sample_tables(group, device, device_ref, offset_ref, give_ref, take_ref):
    shape = (512, 128)
    offsets = offset_ref[...]
    sources = device_ref[...]
    here = offsets // 64 == group
    mine = jnp.where(here, 1.0, 0.0)
    square = (128, 128)
    first = lax.broadcasted_iota(jnp.int32, square, 0)
    second = lax.broadcasted_iota(jnp.int32, square, 1)
    before = jnp.where(first < second, 1.0, 0.0).astype(jnp.bfloat16)
    ones = jnp.ones(square, jnp.bfloat16)

    def plain(a, b):
        return lax.dot_general(
            a.astype(jnp.bfloat16),
            b.astype(jnp.bfloat16),
            (((1,), (0,)), ((), ())),
            preferred_element_type=jnp.float32,
        )

    wide = (512, 512)
    later = lax.broadcasted_iota(jnp.int32, wide, 0)
    earlier = lax.broadcasted_iota(jnp.int32, wide, 1)
    lines = jnp.where((later // 4 == earlier // 4) & (earlier < later), 1.0, 0.0)
    rank = plain(mine, before) + plain(lines, plain(mine, ones))
    value = (sources * 8192 + offsets + 1).astype(jnp.float32)
    lanes = lax.broadcasted_iota(jnp.int32, shape, 1)
    found = jnp.zeros(shape, jnp.float32)
    for k in range(8):
        chosen = jnp.where(here & (rank == float(k)), value, 0.0)
        found = jnp.where(lanes == k, jnp.sum(chosen, axis=1, keepdims=True), found)
    blocks = jnp.where(
        lax.broadcasted_iota(jnp.int32, shape, 0) // 4
        == lax.broadcasted_iota(jnp.int32, shape, 1),
        1.0,
        0.0,
    )
    slots = dot_exact(found, blocks, ((0,), (0,)))[0:8, :].astype(jnp.int32)
    full = slots - 1
    source = full // 8192
    offset = full % 8192
    natural = jnp.zeros_like(full)
    for link in range(6):
        step = STEPS[link]
        sign = jnp.zeros_like(full)
        for bit in range(7):
            if step >> bit & 1:
                sign = sign + (source // (1 << bit)) % 2
        natural = natural + (sign % 2) * (1 << (5 - link))
    part = 2 * ((offset // 8) % 8) + (source // (1 << CORE_BIT)) % 2
    spot = jnp.zeros_like(full)
    for number in range(16):
        turn = FIRST[number]
        turned = (natural % (1 << (6 - turn))) * (1 << turn) + natural // (1 << (6 - turn))
        spot = jnp.where(part == number, turned, spot)
    row = part * 512 + spot * 8 + offset % 8
    give_ref[...] = jnp.clip(jnp.where(slots > 0, row, 8192), 0, 8192)

    total = jnp.zeros(square, jnp.float32)
    for q in range(4):
        groups = offset_ref[pl.ds(4 * device + q, 1), :] // 64
        same = jnp.where(groups == first, 1.0, 0.0)
        count = plain(same, before) + total
        place = jnp.sum(same * count, axis=0, keepdims=True)
        take_ref[q : q + 1, :] = jnp.clip(groups * 8 + place.astype(jnp.int32), 0, 1023)
        total = total + plain(same, ones)


def kernel(
    features_ref,
    bits_hbm,
    device_hbm,
    offset_hbm,
    sketch,
    inverse,
    upper_ref,
    bits_ref,
    device_ref,
    offset_ref,
    rows_in,
    signs,
    core_send,
    core_keep,
    core_got,
    send,
    keep,
    got,
    held,
    give_v,
    take_v,
    give,
    take,
    outgoing,
    received,
    gram_part,
    gram_got,
    gram_row,
    gram,
    work,
    in_sem,
    table_sem,
    core_send_sem,
    core_got_sem,
    send_sem,
    got_sem,
    row_sem,
    sum_sem,
):
    device = lax.axis_index("exa") * 16 + lax.axis_index("exb")
    group = group_of(device)
    partners = [flip(device, 1 << CORE_BIT)] + [flip(device, step) for step in STEPS]
    core_sign = (1 - 2 * bit_of(group, CORE_BIT)).astype(jnp.float32)
    link_sign = [(1 - 2 * bit_of(group, bit)).astype(jnp.float32) for bit in GROUP_BITS]

    loads = [
        pltpu.make_async_copy(
            features_ref.at[pl.ds(1024 * c, 1024)], rows_in.at[pl.ds(1024 * c, 1024)], in_sem.at[c]
        )
        for c in range(8)
    ]
    small = [
        pltpu.make_async_copy(bits_hbm, bits_ref, in_sem.at[8]),
        pltpu.make_async_copy(device_hbm, device_ref, in_sem.at[9]),
        pltpu.make_async_copy(offset_hbm, offset_ref, in_sem.at[10]),
    ]
    small[0].start()
    for load in loads:
        load.start()
    small[1].start()
    small[2].start()
    barrier = pltpu.get_barrier_semaphore()
    for partner in partners:
        pl.semaphore_signal(barrier, inc=1, device_id=place_of(partner), device_id_type=MESH)

    small[0].wait()
    bits = (2 * bits_ref[...] - 1).astype(jnp.float32)
    signs[...] = jnp.transpose(jnp.concatenate([bits, bits], axis=0))

    def first_pass(pair):
        def body(low, carry):
            turned = signs[...]
            for half in range(2):
                tiles = []
                for side in range(2):
                    base = pl.multiple_of(2048 * pair + 1024 * side + 128 * low + 64 * half, 64)
                    column = 0
                    some = []
                    for t in range(8):
                        sign = jnp.broadcast_to(
                            turned[64 * half + 8 * t : 64 * half + 8 * t + 8, 8 * side : 8 * side + 1], (8, 128)
                        )
                        some.append(rows_in[pl.ds(pl.multiple_of(base + 8 * t, 8), 8), :] * sign)
                    for step in (1, 2, 4):
                        for t in range(8):
                            if not t & step:
                                a, b = some[t], some[t + step]
                                some[t], some[t + step] = a + b, a - b
                    tiles.append(some)
                spot = 16 * pair + 2 * low + half
                for t in range(8):
                    a, b = tiles[0][t], core_sign * tiles[1][t]
                    core_keep[t, spot] = a + b
                    core_send[t, spot] = a - b
            signs[...] = pltpu.roll(turned, 127, 1)
            return carry

        lax.fori_loop(0, 8, body, 0)

    def core_copy(part):
        return pltpu.make_async_remote_copy(
            src_ref=core_send.at[part],
            dst_ref=core_got.at[part],
            send_sem=core_send_sem.at[part],
            recv_sem=core_got_sem.at[part],
            device_id=place_of(partners[0]),
            device_id_type=MESH,
        )

    for pair in range(4):
        loads[2 * pair].wait()
        loads[2 * pair + 1].wait()
        first_pass(pair)
        if pair < 3:
            signs[...] = pltpu.roll(signs[...], 120, 1)
    pl.semaphore_wait(barrier, 7)
    for part in range(8):
        core_copy(part).start()

    def link_copy(part, stage):
        link = (FIRST[part] + stage - 1) % 6
        return pltpu.make_async_remote_copy(
            src_ref=send.at[part, stage - 1],
            dst_ref=got.at[part, stage - 1],
            send_sem=send_sem.at[part, stage - 1],
            recv_sem=got_sem.at[part, stage - 1],
            device_id=place_of(partners[1 + link]),
            device_id_type=MESH,
        )

    give_copy = pltpu.make_async_copy(give_v, give, table_sem.at[0])
    take_copy = pltpu.make_async_copy(take_v, take, table_sem.at[1])

    lines = lax.broadcasted_iota(jnp.int32, (8, 128), 0)

    def core_stage(part, side):
        number = 2 * part + side
        turn = FIRST[number]
        sign = link_sign[turn]

        def one(rot):
            spot = rot // (1 << turn) + (rot % (1 << turn)) * (1 << (6 - turn))
            a, b = core_keep[part, spot], core_got[part, spot]
            return a + b if side == 0 else core_sign * (a - b)

        def body(step, carry):
            for more in range(4):
                j = 4 * step + more
                a, b = one(j), sign * one(j + 32)
                keep[number, 0, j] = a + b
                send[number, 0, j] = a - b
            return carry

        lax.fori_loop(0, 8, body, 0)

    def link_stage(part, stage):
        link = (FIRST[part] + stage - 1) % 6
        sign, after = link_sign[link], link_sign[(link + 1) % 6]
        old, new = (stage - 1) % 2, stage % 2

        def pair(i):
            a, b = keep[part, old, i], got[part, stage - 1, i]
            return a + b, sign * (a - b)

        def body(step, carry):
            for more in range(4):
                i = 4 * step + more
                for side, (a, b) in enumerate(zip(pair(i), pair(i + 16))):
                    if stage == 2:
                        a, b = sublane_hadamard(a, lines), sublane_hadamard(b, lines)
                    b = after * b
                    keep[part, new, 2 * i + side] = a + b
                    send[part, stage, 2 * i + side] = a - b
            return carry

        lax.fori_loop(0, 4, body, 0)

    def last_stage(part):
        sign = link_sign[(FIRST[part] + 5) % 6] * SCALE

        def body(step, carry):
            for more in range(4):
                i = 4 * step + more
                a, b = keep[part, 1, i], got[part, 5, i]
                base = pl.multiple_of(512 * part + 16 * i, 16)
                held[pl.ds(base, 8), :] = SCALE * (a + b)
                held[pl.ds(pl.multiple_of(base + 8, 8), 8), :] = sign * (a - b)
            return carry

        lax.fori_loop(0, 8, body, 0)

    for number, (part, stage) in enumerate(ORDER):
        if stage == 0:
            core_copy(part).wait_recv()
            for side in range(2):
                core_stage(part, side)
                link_copy(2 * part + side, 1).start()
        else:
            link_copy(part, stage).wait_recv()
            if stage < 6:
                link_stage(part, stage)
                link_copy(part, stage + 1).start()
            else:
                last_stage(part)
        if number == 7:
            small[1].wait()
            small[2].wait()
            sample_tables(group, device, device_ref, offset_ref, give_v, take_v)
            give_copy.start()
            take_copy.start()
    held[8192:8200, :] = jnp.zeros((8, 128), jnp.float32)
    give_copy.wait()
    take_copy.wait()

    for quarter in range(4):
        for to in range(32 * quarter, 32 * quarter + 32):
            for k in range(8):
                spot = 8 * to + k
                outgoing[spot : spot + 1, :] = held[pl.ds(give[k, to], 1), :]
        some = outgoing[256 * quarter : 256 * quarter + 256, :]
        more = dot_exact(some, some, ((0,), (0,)))
        total = more if quarter == 0 else total + more
    gram_part[...] = total

    def row_copy(to):
        return pltpu.make_async_remote_copy(
            src_ref=outgoing.at[pl.ds(pl.multiple_of(8 * to, 8), 8)],
            dst_ref=received.at[pl.ds(pl.multiple_of(8 * group, 8), 8)],
            send_sem=row_sem.at[0],
            recv_sem=row_sem.at[1],
            device_id=place_of(to),
            device_id_type=MESH,
        )

    def part_copy(to):
        return pltpu.make_async_remote_copy(
            src_ref=gram_part.at[pl.ds(to, 1)],
            dst_ref=gram_got.at[pl.ds(device, 1)],
            send_sem=sum_sem.at[0],
            recv_sem=sum_sem.at[1],
            device_id=place_of(to),
            device_id_type=MESH,
        )

    def sum_copy(to):
        return pltpu.make_async_remote_copy(
            src_ref=gram_row,
            dst_ref=gram.at[pl.ds(device, 1)],
            send_sem=sum_sem.at[2],
            recv_sem=sum_sem.at[3],
            device_id=place_of(to),
            device_id_type=MESH,
        )

    exa, exb = lax.axis_index("exa"), lax.axis_index("exb")
    turns = (2, 3, 1, 0)
    lower = {dz: 32 * ((exa // 2 + dz) % 4) for dz in turns}
    middle = {dx: 4 * ((exb // 4 + dx) % 4) for dx in turns}
    upper = {dy: (exb + dy) % 4 for dy in turns}
    cores = (16 * (1 - exa % 2), 16 * (exa % 2))
    shifts = [(z, x, y, c) for z in turns for x in turns for y in turns for c in (0, 1)]
    shifts = sorted(shifts, key=lambda t: -sum(min(v, 4 - v) for v in t[:3]))

    def all_others(copy):
        for z, x, y, c in shifts[:-1]:
            copy(lower[z] + cores[c] + (middle[x] + upper[y])).start()

    def wait_bytes(ref, sem):
        pltpu.make_async_copy(ref, ref, sem).wait()

    all_others(part_copy)
    gram_got[pl.ds(device, 1), :] = gram_part[pl.ds(device, 1), :]
    wait_bytes(gram_got.at[pl.ds(0, 127)], sum_sem.at[1])
    gram_row[...] = jnp.sum(gram_got[...], axis=0, keepdims=True) * (1.0 / 65536.0)
    all_others(sum_copy)
    gram[pl.ds(device, 1), :] = gram_row[...]
    all_others(row_copy)
    received[pl.ds(pl.multiple_of(8 * group, 8), 8), :] = outgoing[
        pl.ds(pl.multiple_of(8 * device, 8), 8), :
    ]

    def take_rows(panel):
        if panel == 6:
            wait_bytes(received.at[pl.ds(0, 1016)], row_sem.at[1])
        if panel >= 6:
            for j in range(256 * (panel - 6), 256 * (panel - 5)):
                row = take[j // 128, j % 128]
                sketch[j : j + 1, :] = received[pl.ds(row, 1), :]

    wait_bytes(gram.at[pl.ds(0, 127)], sum_sem.at[3])
    factor(gram[...], upper_ref, inverse, work, take_rows)

    for part in range(8):
        core_copy(part).wait_send()
    for part in range(16):
        for stage in range(1, 7):
            link_copy(part, stage).wait_send()
    wait_bytes(outgoing.at[pl.ds(0, 1016)], row_sem.at[0])
    wait_bytes(gram_part.at[pl.ds(0, 127)], sum_sem.at[0])
    wait_bytes(gram_part.at[pl.ds(0, 127)], sum_sem.at[2])


def finish(sketch_ref, inverse_ref, factor_ref, q_ref, upper_ref):
    upper_ref[...] = factor_ref[...]
    q_ref[...] = dot_exact(sketch_ref[...], inverse_ref[...], ((1,), (1,)))


def per_device(features, sign_bits, sample_device, sample_offset):
    f32, i32 = jnp.float32, jnp.int32
    dma = pltpu.SemaphoreType.DMA
    sketch, inverse, upper = pl.pallas_call(
        kernel,
        out_shape=[
            jax.ShapeDtypeStruct((512, 128), f32),
            jax.ShapeDtypeStruct((128, 128), f32),
            jax.ShapeDtypeStruct((128, 128), f32),
        ],
        in_specs=[pl.BlockSpec(memory_space=pltpu.HBM)] * 4,
        out_specs=[pl.BlockSpec(memory_space=pltpu.VMEM)] * 3,
        scratch_shapes=[
            pltpu.VMEM((64, 128), i32),
            pltpu.VMEM((512, 128), i32),
            pltpu.VMEM((512, 128), i32),
            pltpu.VMEM((8192, 128), f32),
            pltpu.VMEM((128, 128), f32),
            pltpu.VMEM((8, 64, 8, 128), f32),
            pltpu.VMEM((8, 64, 8, 128), f32),
            pltpu.VMEM((8, 64, 8, 128), f32),
            pltpu.VMEM((16, 6, 32, 8, 128), f32),
            pltpu.VMEM((16, 2, 32, 8, 128), f32),
            pltpu.VMEM((16, 6, 32, 8, 128), f32),
            pltpu.VMEM((8200, 128), f32),
            pltpu.VMEM((8, 128), i32),
            pltpu.VMEM((8, 128), i32),
            pltpu.SMEM((8, 128), i32),
            pltpu.SMEM((8, 128), i32),
            pltpu.VMEM((1024, 128), f32),
            pltpu.VMEM((1024, 128), f32),
            pltpu.VMEM((128, 128), f32),
            pltpu.VMEM((128, 128), f32),
            pltpu.VMEM((1, 128), f32),
            pltpu.VMEM((128, 128), f32),
            pltpu.VMEM((128, 256), f32),
            dma((11,)),
            dma((2,)),
            dma((8,)),
            dma((8,)),
            dma((16, 6)),
            dma((16, 6)),
            dma((2,)),
            dma((4,)),
        ],
        compiler_params=pltpu.CompilerParams(
            collective_id=0, has_side_effects=True, vmem_limit_bytes=50 * 2**20
        ),
    )(
        features,
        *[pltpu.with_memory_space_constraint(a, pltpu.HBM) for a in (sign_bits.reshape(64, 128), sample_device.reshape(512, 128), sample_offset.reshape(512, 128))],
    )
    return pl.pallas_call(
        finish,
        out_shape=[
            jax.ShapeDtypeStruct((512, 128), f32),
            jax.ShapeDtypeStruct((128, 128), f32),
        ],
        compiler_params=pltpu.CompilerParams(vmem_limit_bytes=8 * 2**20),
    )(sketch, inverse, upper)


def solution(mesh):
    placed = (P(("exa", "exb"), None), P(("exa", "exb")), P(), P())
    return jax.shard_map(
        per_device,
        mesh=mesh,
        in_specs=placed,
        out_specs=(P(("exa", "exb"), None), P()),
        check_vma=False,
    )
```

```python
import jax
import jax.numpy as jnp
from jax import lax
from jax.experimental import pallas as pl
from jax.experimental.pallas import tpu as pltpu
from jax.sharding import PartitionSpec as P

MESH = pl.DeviceIdType.MESH
GROUP_BITS = (6, 5, 3, 2, 1, 0)
STEPS = (96, 32, 12, 4, 3, 1)
CORE_BIT = 4
FIRST = (0, 2, 4, 1, 3, 5, 0, 2, 4, 1, 3, 5, 0, 2, 4, 1)
ORDER = (
    (0, 0), (1, 0), (2, 0), (3, 0), (4, 0), (5, 0), (6, 0), (7, 0), (0, 1), (1, 1),
    (2, 1), (3, 1), (4, 1), (5, 1), (6, 1), (7, 1), (8, 1), (9, 1), (10, 1), (11, 1),
    (12, 1), (13, 1), (14, 1), (15, 1), (1, 2), (2, 2), (5, 2), (3, 2), (4, 2), (0, 2),
    (7, 2), (8, 2), (11, 2), (9, 2), (10, 2), (6, 2), (13, 2), (14, 2), (2, 3), (15, 2),
    (1, 3), (12, 2), (3, 3), (4, 3), (8, 3), (0, 3), (7, 3), (5, 3), (9, 3), (10, 3),
    (14, 3), (6, 3), (13, 3), (11, 3), (15, 3), (1, 4), (4, 4), (12, 3), (3, 4), (2, 4),
    (0, 4), (7, 4), (10, 4), (5, 4), (9, 4), (8, 4), (6, 4), (13, 4), (1, 5), (11, 4),
    (15, 4), (14, 4), (12, 4), (3, 5), (7, 5), (2, 5), (0, 5), (4, 5), (5, 5), (9, 5),
    (13, 5), (8, 5), (6, 5), (10, 5), (11, 5), (15, 5), (3, 6), (14, 5), (12, 5), (1, 6),
    (2, 6), (0, 6), (9, 6), (4, 6), (5, 6), (7, 6), (8, 6), (6, 6), (15, 6), (10, 6),
    (11, 6), (13, 6), (14, 6), (12, 6),
)
SCALE = 1.0 / 1024.0


def bit_of(number, bit):
    return (number // (1 << bit)) % 2


def flip(number, mask):
    for bit in range(7):
        if mask >> bit & 1:
            number = number + (1 << bit) * (1 - 2 * bit_of(number, bit))
    return number


def group_of(device):
    out = 0
    for bit in range(7):
        value = bit_of(device, bit)
        if bit in (0, 2, 5):
            above = bit_of(device, bit + 1)
            value = value + above - 2 * value * above
        out = out + value * (1 << bit)
    return out


def place_of(device):
    return (device // 16, device % 16)


def sublane_hadamard(tile, rows):
    for step in (4, 2, 1):
        high = (rows // step) % 2 == 1
        if step == 4:
            other = pltpu.roll(tile, 4, 0)
        else:
            other = jnp.where(high, pltpu.roll(tile, step, 0), pltpu.roll(tile, 8 - step, 0))
        tile = jnp.where(high, other - tile, tile + other)
    return tile


def factor(gram, upper_ref, inverse_ref, work, beside):
    width, size = 128, 16
    rows = lax.broadcasted_iota(jnp.int32, (8, width), 0)
    lanes = lax.broadcasted_iota(jnp.int32, (8, width), 1)
    work[:, :width] = gram
    work[:, width:] = (
        lax.broadcasted_iota(jnp.int32, (width, width), 0)
        == lax.broadcasted_iota(jnp.int32, (width, width), 1)
    ).astype(jnp.float32)
    both = work[:size, :]
    for panel in range(width // size):
        beside(panel)
        low, end = size * panel, size * (panel + 1)
        left = [both[8 * t : 8 * t + 8, :width] for t in range(2)]
        right = [both[8 * t : 8 * t + 8, width:] for t in range(2)]
        cols = [
            [jnp.broadcast_to(tile[:, low + j : low + j + 1], (8, width)) for tile in left]
            for j in range(size)
        ]
        pivots = [jnp.ones((8, width), jnp.float32) for _ in range(2)]
        for i in range(size):
            own, row = divmod(i, 8)
            pivot = jnp.broadcast_to(cols[i][own][row : row + 1, :], (8, width))
            pivots[own] = jnp.where(rows == row, pivot, pivots[own])
            left_row, right_row = left[own][row : row + 1, :], right[own][row : row + 1, :]
            col_row = [cols[j][own][row : row + 1, :] for j in range(size)]
            for t in range(own, 2):
                if t == own and row == 7:
                    continue
                scaled = cols[i][t] / pivot
                if t == own:
                    scaled = jnp.where(rows > row, scaled, 0.0)
                for j in range(i + 1, size):
                    cols[j][t] = cols[j][t] - scaled * col_row[j]
                left[t] = left[t] - scaled * left_row
                right[t] = right[t] - scaled * right_row
        for t in range(2):
            root = lax.rsqrt(pivots[t])
            root = root * (1.5 - 0.5 * pivots[t] * root * root)
            left[t] = jnp.where(lanes >= rows + (low + 8 * t), left[t] * root, 0.0)
            right[t] = right[t] * root
            upper_ref[low + 8 * t : low + 8 * t + 8, :] = left[t]
            inverse_ref[low + 8 * t : low + 8 * t + 8, :] = right[t]
        if end < width:
            top = jnp.concatenate(left, axis=0)
            turned = top.T
            top = jnp.concatenate([top, jnp.concatenate(right, axis=0)], axis=1)
            both = work[end : end + size, :] - dot_exact(turned[end : end + size, :], top, ((1,), (0,)))
            if end + size < width:
                work[end + size :, :] = work[end + size :, :] - dot_exact(
                    turned[end + size :, :], top, ((1,), (0,))
                )


def dot_exact(a, b, contract):
    return lax.dot_general(
        a,
        b,
        (contract, ((), ())),
        precision=lax.Precision.HIGHEST,
        preferred_element_type=jnp.float32,
    )


def sample_tables(group, device, device_ref, offset_ref, give_ref, take_ref):
    shape = (512, 128)
    offsets = offset_ref[...]
    sources = device_ref[...]
    here = offsets // 64 == group
    mine = jnp.where(here, 1.0, 0.0)
    square = (128, 128)
    first = lax.broadcasted_iota(jnp.int32, square, 0)
    second = lax.broadcasted_iota(jnp.int32, square, 1)
    before = jnp.where(first < second, 1.0, 0.0).astype(jnp.bfloat16)
    ones = jnp.ones(square, jnp.bfloat16)

    def plain(a, b):
        return lax.dot_general(
            a.astype(jnp.bfloat16),
            b.astype(jnp.bfloat16),
            (((1,), (0,)), ((), ())),
            preferred_element_type=jnp.float32,
        )

    wide = (512, 512)
    later = lax.broadcasted_iota(jnp.int32, wide, 0)
    earlier = lax.broadcasted_iota(jnp.int32, wide, 1)
    lines = jnp.where((later // 4 == earlier // 4) & (earlier < later), 1.0, 0.0)
    rank = plain(mine, before) + plain(lines, plain(mine, ones))
    value = (sources * 8192 + offsets + 1).astype(jnp.float32)
    lanes = lax.broadcasted_iota(jnp.int32, shape, 1)
    found = jnp.zeros(shape, jnp.float32)
    for k in range(8):
        chosen = jnp.where(here & (rank == float(k)), value, 0.0)
        found = jnp.where(lanes == k, jnp.sum(chosen, axis=1, keepdims=True), found)
    blocks = jnp.where(
        lax.broadcasted_iota(jnp.int32, shape, 0) // 4
        == lax.broadcasted_iota(jnp.int32, shape, 1),
        1.0,
        0.0,
    )
    slots = dot_exact(found, blocks, ((0,), (0,)))[0:8, :].astype(jnp.int32)
    full = slots - 1
    source = full // 8192
    offset = full % 8192
    natural = jnp.zeros_like(full)
    for link in range(6):
        step = STEPS[link]
        sign = jnp.zeros_like(full)
        for bit in range(7):
            if step >> bit & 1:
                sign = sign + (source // (1 << bit)) % 2
        natural = natural + (sign % 2) * (1 << (5 - link))
    part = 2 * ((offset // 8) % 8) + (source // (1 << CORE_BIT)) % 2
    spot = jnp.zeros_like(full)
    for number in range(16):
        turn = FIRST[number]
        turned = (natural % (1 << (6 - turn))) * (1 << turn) + natural // (1 << (6 - turn))
        spot = jnp.where(part == number, turned, spot)
    row = part * 512 + spot * 8 + offset % 8
    give_ref[...] = jnp.clip(jnp.where(slots > 0, row, 8192), 0, 8192)

    total = jnp.zeros(square, jnp.float32)
    for q in range(4):
        groups = offset_ref[pl.ds(4 * device + q, 1), :] // 64
        same = jnp.where(groups == first, 1.0, 0.0)
        count = plain(same, before) + total
        place = jnp.sum(same * count, axis=0, keepdims=True)
        take_ref[q : q + 1, :] = jnp.clip(groups * 8 + place.astype(jnp.int32), 0, 1023)
        total = total + plain(same, ones)


def kernel(
    features_ref,
    bits_hbm,
    device_hbm,
    offset_hbm,
    sketch,
    inverse,
    upper_ref,
    bits_ref,
    device_ref,
    offset_ref,
    rows_in,
    signs,
    core_send,
    core_keep,
    core_got,
    send,
    keep,
    got,
    held,
    give_v,
    take_v,
    give,
    take,
    outgoing,
    received,
    gram_part,
    gram_got,
    gram_row,
    gram,
    work,
    in_sem,
    table_sem,
    core_send_sem,
    core_got_sem,
    send_sem,
    got_sem,
    row_sem,
    sum_sem,
):
    device = lax.axis_index("exa") * 16 + lax.axis_index("exb")
    group = group_of(device)
    partners = [flip(device, 1 << CORE_BIT)] + [flip(device, step) for step in STEPS]
    core_sign = (1 - 2 * bit_of(group, CORE_BIT)).astype(jnp.float32)
    link_sign = [(1 - 2 * bit_of(group, bit)).astype(jnp.float32) for bit in GROUP_BITS]

    loads = [
        pltpu.make_async_copy(
            features_ref.at[pl.ds(1024 * c, 1024)], rows_in.at[pl.ds(1024 * c, 1024)], in_sem.at[c]
        )
        for c in range(8)
    ]
    small = [
        pltpu.make_async_copy(bits_hbm, bits_ref, in_sem.at[8]),
        pltpu.make_async_copy(device_hbm, device_ref, in_sem.at[9]),
        pltpu.make_async_copy(offset_hbm, offset_ref, in_sem.at[10]),
    ]
    small[0].start()
    for load in loads:
        load.start()
    small[1].start()
    small[2].start()
    barrier = pltpu.get_barrier_semaphore()
    for partner in partners:
        pl.semaphore_signal(barrier, inc=1, device_id=place_of(partner), device_id_type=MESH)

    small[0].wait()
    bits = (2 * bits_ref[...] - 1).astype(jnp.float32)
    signs[...] = jnp.transpose(jnp.concatenate([bits, bits], axis=0))

    def first_pass(pair):
        def body(low, carry):
            turned = signs[...]
            for half in range(2):
                tiles = []
                for side in range(2):
                    base = pl.multiple_of(2048 * pair + 1024 * side + 128 * low + 64 * half, 64)
                    column = 0
                    some = []
                    for t in range(8):
                        sign = jnp.broadcast_to(
                            turned[64 * half + 8 * t : 64 * half + 8 * t + 8, 8 * side : 8 * side + 1], (8, 128)
                        )
                        some.append(rows_in[pl.ds(pl.multiple_of(base + 8 * t, 8), 8), :] * sign)
                    for step in (1, 2, 4):
                        for t in range(8):
                            if not t & step:
                                a, b = some[t], some[t + step]
                                some[t], some[t + step] = a + b, a - b
                    tiles.append(some)
                spot = 16 * pair + 2 * low + half
                for t in range(8):
                    a, b = tiles[0][t], core_sign * tiles[1][t]
                    core_keep[t, spot] = a + b
                    core_send[t, spot] = a - b
            signs[...] = pltpu.roll(turned, 127, 1)
            return carry

        lax.fori_loop(0, 8, body, 0)

    def core_copy(part):
        return pltpu.make_async_remote_copy(
            src_ref=core_send.at[part],
            dst_ref=core_got.at[part],
            send_sem=core_send_sem.at[part],
            recv_sem=core_got_sem.at[part],
            device_id=place_of(partners[0]),
            device_id_type=MESH,
        )

    for pair in range(4):
        loads[2 * pair].wait()
        loads[2 * pair + 1].wait()
        first_pass(pair)
        if pair < 3:
            signs[...] = pltpu.roll(signs[...], 120, 1)
    pl.semaphore_wait(barrier, 7)
    for part in range(8):
        core_copy(part).start()

    def link_copy(part, stage):
        link = (FIRST[part] + stage - 1) % 6
        return pltpu.make_async_remote_copy(
            src_ref=send.at[part, stage - 1],
            dst_ref=got.at[part, stage - 1],
            send_sem=send_sem.at[part, stage - 1],
            recv_sem=got_sem.at[part, stage - 1],
            device_id=place_of(partners[1 + link]),
            device_id_type=MESH,
        )

    give_copy = pltpu.make_async_copy(give_v, give, table_sem.at[0])
    take_copy = pltpu.make_async_copy(take_v, take, table_sem.at[1])

    lines = lax.broadcasted_iota(jnp.int32, (8, 128), 0)

    def core_stage(part, side):
        number = 2 * part + side
        turn = FIRST[number]
        sign = link_sign[turn]

        def one(rot):
            spot = rot // (1 << turn) + (rot % (1 << turn)) * (1 << (6 - turn))
            a, b = core_keep[part, spot], core_got[part, spot]
            return a + b if side == 0 else core_sign * (a - b)

        def body(step, carry):
            for more in range(4):
                j = 4 * step + more
                a, b = one(j), sign * one(j + 32)
                keep[number, 0, j] = a + b
                send[number, 0, j] = a - b
            return carry

        lax.fori_loop(0, 8, body, 0)

    def link_stage(part, stage):
        link = (FIRST[part] + stage - 1) % 6
        sign, after = link_sign[link], link_sign[(link + 1) % 6]
        old, new = (stage - 1) % 2, stage % 2

        def pair(i):
            a, b = keep[part, old, i], got[part, stage - 1, i]
            return a + b, sign * (a - b)

        def body(step, carry):
            for more in range(8):
                i = 8 * step + more
                for side, (a, b) in enumerate(zip(pair(i), pair(i + 16))):
                    if stage == 2:
                        a, b = sublane_hadamard(a, lines), sublane_hadamard(b, lines)
                    b = after * b
                    keep[part, new, 2 * i + side] = a + b
                    send[part, stage, 2 * i + side] = a - b
            return carry

        lax.fori_loop(0, 2, body, 0)

    def last_stage(part):
        sign = link_sign[(FIRST[part] + 5) % 6] * SCALE

        def body(step, carry):
            for more in range(4):
                i = 4 * step + more
                a, b = keep[part, 1, i], got[part, 5, i]
                base = pl.multiple_of(512 * part + 16 * i, 16)
                held[pl.ds(base, 8), :] = SCALE * (a + b)
                held[pl.ds(pl.multiple_of(base + 8, 8), 8), :] = sign * (a - b)
            return carry

        lax.fori_loop(0, 8, body, 0)

    for number, (part, stage) in enumerate(ORDER):
        if stage == 0:
            core_copy(part).wait_recv()
            for side in range(2):
                core_stage(part, side)
                link_copy(2 * part + side, 1).start()
        else:
            link_copy(part, stage).wait_recv()
            if stage < 6:
                link_stage(part, stage)
                link_copy(part, stage + 1).start()
            else:
                last_stage(part)
        if number == 7:
            small[1].wait()
            small[2].wait()
            sample_tables(group, device, device_ref, offset_ref, give_v, take_v)
            give_copy.start()
            take_copy.start()
    held[8192:8200, :] = jnp.zeros((8, 128), jnp.float32)
    give_copy.wait()
    take_copy.wait()

    for quarter in range(4):
        for to in range(32 * quarter, 32 * quarter + 32):
            for k in range(8):
                spot = 8 * to + k
                outgoing[spot : spot + 1, :] = held[pl.ds(give[k, to], 1), :]
        some = outgoing[256 * quarter : 256 * quarter + 256, :]
        more = dot_exact(some, some, ((0,), (0,)))
        total = more if quarter == 0 else total + more
    gram_part[...] = total

    def row_copy(to):
        return pltpu.make_async_remote_copy(
            src_ref=outgoing.at[pl.ds(pl.multiple_of(8 * to, 8), 8)],
            dst_ref=received.at[pl.ds(pl.multiple_of(8 * group, 8), 8)],
            send_sem=row_sem.at[0],
            recv_sem=row_sem.at[1],
            device_id=place_of(to),
            device_id_type=MESH,
        )

    def part_copy(to):
        return pltpu.make_async_remote_copy(
            src_ref=gram_part.at[pl.ds(to, 1)],
            dst_ref=gram_got.at[pl.ds(device, 1)],
            send_sem=sum_sem.at[0],
            recv_sem=sum_sem.at[1],
            device_id=place_of(to),
            device_id_type=MESH,
        )

    def sum_copy(to):
        return pltpu.make_async_remote_copy(
            src_ref=gram_row,
            dst_ref=gram.at[pl.ds(device, 1)],
            send_sem=sum_sem.at[2],
            recv_sem=sum_sem.at[3],
            device_id=place_of(to),
            device_id_type=MESH,
        )

    exa, exb = lax.axis_index("exa"), lax.axis_index("exb")
    turns = (2, 3, 1, 0)
    lower = {dz: 32 * ((exa // 2 + dz) % 4) for dz in turns}
    middle = {dx: 4 * ((exb // 4 + dx) % 4) for dx in turns}
    upper = {dy: (exb + dy) % 4 for dy in turns}
    cores = (16 * (1 - exa % 2), 16 * (exa % 2))
    shifts = [(z, x, y, c) for z in turns for x in turns for y in turns for c in (0, 1)]
    shifts = sorted(shifts, key=lambda t: -sum(min(v, 4 - v) for v in t[:3]))

    def all_others(copy):
        for z, x, y, c in shifts[:-1]:
            copy(lower[z] + cores[c] + (middle[x] + upper[y])).start()

    def wait_bytes(ref, sem):
        pltpu.make_async_copy(ref, ref, sem).wait()

    all_others(part_copy)
    gram_got[pl.ds(device, 1), :] = gram_part[pl.ds(device, 1), :]
    wait_bytes(gram_got.at[pl.ds(0, 127)], sum_sem.at[1])
    gram_row[...] = jnp.sum(gram_got[...], axis=0, keepdims=True) * (1.0 / 65536.0)
    all_others(sum_copy)
    gram[pl.ds(device, 1), :] = gram_row[...]
    all_others(row_copy)
    received[pl.ds(pl.multiple_of(8 * group, 8), 8), :] = outgoing[
        pl.ds(pl.multiple_of(8 * device, 8), 8), :
    ]

    def take_rows(panel):
        if panel == 6:
            wait_bytes(received.at[pl.ds(0, 1016)], row_sem.at[1])
        if panel >= 6:
            for j in range(256 * (panel - 6), 256 * (panel - 5)):
                row = take[j // 128, j % 128]
                sketch[j : j + 1, :] = received[pl.ds(row, 1), :]

    wait_bytes(gram.at[pl.ds(0, 127)], sum_sem.at[3])
    factor(gram[...], upper_ref, inverse, work, take_rows)

    for part in range(8):
        core_copy(part).wait_send()
    for part in range(16):
        for stage in range(1, 7):
            link_copy(part, stage).wait_send()
    wait_bytes(outgoing.at[pl.ds(0, 1016)], row_sem.at[0])
    wait_bytes(gram_part.at[pl.ds(0, 127)], sum_sem.at[0])
    wait_bytes(gram_part.at[pl.ds(0, 127)], sum_sem.at[2])


def finish(sketch_ref, inverse_ref, factor_ref, q_ref, upper_ref):
    upper_ref[...] = factor_ref[...]
    q_ref[...] = dot_exact(sketch_ref[...], inverse_ref[...], ((1,), (1,)))


def per_device(features, sign_bits, sample_device, sample_offset):
    f32, i32 = jnp.float32, jnp.int32
    dma = pltpu.SemaphoreType.DMA
    sketch, inverse, upper = pl.pallas_call(
        kernel,
        out_shape=[
            jax.ShapeDtypeStruct((512, 128), f32),
            jax.ShapeDtypeStruct((128, 128), f32),
            jax.ShapeDtypeStruct((128, 128), f32),
        ],
        in_specs=[pl.BlockSpec(memory_space=pltpu.HBM)] * 4,
        out_specs=[pl.BlockSpec(memory_space=pltpu.VMEM)] * 3,
        scratch_shapes=[
            pltpu.VMEM((64, 128), i32),
            pltpu.VMEM((512, 128), i32),
            pltpu.VMEM((512, 128), i32),
            pltpu.VMEM((8192, 128), f32),
            pltpu.VMEM((128, 128), f32),
            pltpu.VMEM((8, 64, 8, 128), f32),
            pltpu.VMEM((8, 64, 8, 128), f32),
            pltpu.VMEM((8, 64, 8, 128), f32),
            pltpu.VMEM((16, 6, 32, 8, 128), f32),
            pltpu.VMEM((16, 2, 32, 8, 128), f32),
            pltpu.VMEM((16, 6, 32, 8, 128), f32),
            pltpu.VMEM((8200, 128), f32),
            pltpu.VMEM((8, 128), i32),
            pltpu.VMEM((8, 128), i32),
            pltpu.SMEM((8, 128), i32),
            pltpu.SMEM((8, 128), i32),
            pltpu.VMEM((1024, 128), f32),
            pltpu.VMEM((1024, 128), f32),
            pltpu.VMEM((128, 128), f32),
            pltpu.VMEM((128, 128), f32),
            pltpu.VMEM((1, 128), f32),
            pltpu.VMEM((128, 128), f32),
            pltpu.VMEM((128, 256), f32),
            dma((11,)),
            dma((2,)),
            dma((8,)),
            dma((8,)),
            dma((16, 6)),
            dma((16, 6)),
            dma((2,)),
            dma((4,)),
        ],
        compiler_params=pltpu.CompilerParams(
            collective_id=0, has_side_effects=True, vmem_limit_bytes=50 * 2**20
        ),
    )(
        features,
        *[pltpu.with_memory_space_constraint(a, pltpu.HBM) for a in (sign_bits.reshape(64, 128), sample_device.reshape(512, 128), sample_offset.reshape(512, 128))],
    )
    return pl.pallas_call(
        finish,
        out_shape=[
            jax.ShapeDtypeStruct((512, 128), f32),
            jax.ShapeDtypeStruct((128, 128), f32),
        ],
        compiler_params=pltpu.CompilerParams(vmem_limit_bytes=8 * 2**20),
    )(sketch, inverse, upper)


def solution(mesh):
    placed = (P(("exa", "exb"), None), P(("exa", "exb")), P(), P())
    return jax.shard_map(
        per_device,
        mesh=mesh,
        in_specs=placed,
        out_specs=(P(("exa", "exb"), None), P()),
        check_vma=False,
    )
```
